512 devices in a mesh: pb: 32 (over z, x), ka: 16 (over y, core).
Axes of the slice: x: 4, y: 8, z: 8, core: 2. Of those that a mesh axis runs over, the one named last changes fastest.
Arguments:
- features: bfloat16 [65536, 1024], P(('pb', 'ka')), may hold values from -8.5 to 8.5
- order: int32 [65536], P(('pb', 'ka')), may hold values from 0 to 127, as said below
- neighbours: int32 [512, 24], P('pb'), may hold values from 0 to 511, as said below
- counts: int32 [512], P('pb'), may hold values from 1 to 24, as said below
- qkv_weight: bfloat16 [1024, 1536], P(('pb', 'ka')), may hold values from -0.25 to 0.25
- out_weight: bfloat16 [512, 1024], P(None, ('pb', 'ka')), may hold values from -1 to 1
Outputs:
- mixed: bfloat16 [65536, 1024], P(('pb', 'ka'))
The draws below stay inside these ranges and needn't reach their ends.
Inputs may be any that keep to these rules, and one draw needn't show every extreme that they name: `order`: each aligned group of 128 entries is a permutation of 0 to 127. `neighbours`: entry 0 of the list of block a is a itself; the first counts[a] entries are distinct and lie in a's slab of 16 blocks or in the slabs just before and after it, cyclically; slots from counts[a] on hold some block id and are not part of the list. `counts`: some block's list fills all 24 slots.
All inputs are finite; a program needn't handle non-finite values.
Results may differ from the reference program's by a relative error of at most 0.012.
The reference program's roundings to bfloat16 on the way (of `sorted_rows`, `group_max`, `soft_rounded`, `group_out`, `total_rounded` and `attended`) count: a program that leaves them out, or rounds other values in their place, can miss the bound.
Values may be sent and summed in bfloat16 or wider, within the bound.
No kernel may reach another device: no remote copies, remote signals or barrier semaphores. Data moves between devices by JAX's collectives and lax.ppermute only.
A program may use at most 64 MiB of HBM per device.

```python
import jax
import jax.numpy as jnp
from jax import lax

D = 1024
HEADS = 8
HD = 64
BLK = 128
KB_DEV = 1
RD = 128
SLAB_BLK = 16
QBLOCKS = 512
NP = 65536
NBR_MAX = 24
N_KA = 16


def neighbour_tables(key):
    base_key = jax.random.fold_in(key, 11)
    count_key, slot_key, pick_key = jax.random.split(base_key, 3)
    candidates = 3 * SLAB_BLK
    blocks = jnp.arange(QBLOCKS)
    slab_of = blocks // SLAB_BLK
    own_slot = SLAB_BLK + blocks % SLAB_BLK
    permuted = jax.vmap(lambda sub_key: jax.random.permutation(sub_key, candidates))(jax.random.split(slot_key, QBLOCKS))
    sort_score = jnp.where(permuted == own_slot[:, None], -1, jnp.arange(candidates)[None, :])
    arranged = jnp.argsort(sort_score, axis=1, stable=True)
    ordered = jnp.take_along_axis(permuted, arranged, axis=1)[:, :NBR_MAX]
    slab_count = QBLOCKS // SLAB_BLK
    other_slab = (slab_of[:, None] + ordered // SLAB_BLK - 1) % slab_count
    listed = other_slab * SLAB_BLK + ordered % SLAB_BLK
    count_draw = jax.random.randint(count_key, (QBLOCKS,), 1, NBR_MAX + 1)
    full_block = jax.random.randint(pick_key, (), 0, QBLOCKS)
    count_draw = jnp.where(blocks == full_block, NBR_MAX, count_draw)
    padding = listed[:, NBR_MAX - 1:NBR_MAX]
    listed = jnp.where(jnp.arange(NBR_MAX)[None, :] < count_draw[:, None], listed, padding)
    return (listed.astype(jnp.int32), count_draw.astype(jnp.int32))


def draw_neighbours(key, part):
    return neighbour_tables(key)[0]


def draw_counts(key, part):
    return neighbour_tables(key)[1]


def draw_order(key, part):
    row_groups = NP // RD
    sub_keys = jax.random.split(jax.random.fold_in(key, 3), row_groups)
    permuted = jax.vmap(lambda sub_key: jax.random.permutation(sub_key, RD))(sub_keys)
    return permuted.reshape(-1).astype(jnp.int32)


def draw_features(key, part):
    base_key = jax.random.fold_in(jax.random.fold_in(key, 5), 0)
    drawn = jnp.clip(jax.random.normal(base_key, (NP, D), jnp.float32), -6.0, 6.0)
    return drawn.astype(jnp.bfloat16)


def steps_of(own_key, extent, cuts, low, largest):
    def one(dim, shards_of):
        steps = jax.random.uniform(jax.random.fold_in(jax.random.fold_in(own_key, 6), dim), (shards_of,), jnp.float32, low / len(cuts), largest / len(cuts))
        return jnp.repeat(jnp.exp(steps), extent[dim] // shards_of).reshape((-1,) + (1,) * (len(extent) - dim - 1))

    level = one(*cuts[0])
    for cut in cuts[1:]:
        level = level * one(*cut)
    return level


def normal_values(key, shape, scale, limit, pieces=(), kind=jnp.bfloat16):
    level = steps_of(key, shape, pieces, -0.22, 0.18) if pieces else 1.0
    array = jax.random.normal(key, shape, jnp.float32) * scale * level
    return jnp.minimum(jnp.maximum(array, -limit), limit).astype(kind)


def setup_inputs(seed: int = 0) -> dict:
    key_list = jax.random.split(jax.random.key(seed), 7)
    return {
        "features": draw_features(jax.random.fold_in(key_list[6], 71), 0),
        "order": draw_order(jax.random.fold_in(key_list[6], 71), 0),
        "neighbours": draw_neighbours(jax.random.fold_in(key_list[6], 71), 0),
        "counts": draw_counts(jax.random.fold_in(key_list[6], 71), 0),
        "qkv_weight": normal_values(key_list[4], (D, 3 * HEADS * HD), (D // 2) ** -0.5, 0.25, ((0, 512),)),
        "out_weight": normal_values(key_list[5], (HEADS * HD, D), (HEADS * HD // 16) ** -0.5, 1.0, ((1, 512),)),
    }


def reference(features, order, neighbours, counts, qkv_weight, out_weight):
    dev_rows = BLK * KB_DEV
    row_groups = features.shape[0] // dev_rows
    sorted_rows = jax.vmap(lambda grouped, permuted: grouped[permuted])(
        features.reshape(row_groups, dev_rows, D), order.reshape(row_groups, dev_rows)).reshape(-1, D)
    projected = jnp.dot(sorted_rows, qkv_weight, preferred_element_type=jnp.float32)
    attn_width = HEADS * HD
    queries = projected[:, :attn_width].astype(jnp.bfloat16).reshape(QBLOCKS, BLK, HEADS, HD)
    key_rows = projected[:, attn_width:2 * attn_width].astype(jnp.bfloat16).reshape(QBLOCKS, BLK, HEADS, HD)
    values = projected[:, 2 * attn_width:].astype(jnp.bfloat16).reshape(QBLOCKS, BLK, HEADS, HD)
    score_scale = HD ** -0.5

    def one_block(block_args):
        query_block, listed, count_now = block_args
        listed_slot = jnp.arange(NBR_MAX) < count_now
        owner_group = (listed // KB_DEV) % N_KA
        member = (owner_group[:, None] == jnp.arange(N_KA)[None, :]) & listed_slot[:, None]
        near_keys = key_rows[listed].astype(jnp.float32)
        near_values = values[listed].astype(jnp.float32)
        scores = jnp.einsum('qhd,jkhd->hqjk', query_block.astype(jnp.float32), near_keys) * score_scale
        slot_max = jnp.max(scores, axis=-1)
        group_max = jnp.max(jnp.where(member[None, None], slot_max[..., None], -1e30), axis=2)
        group_max = lax.optimization_barrier(group_max.astype(jnp.bfloat16)).astype(jnp.float32)
        slot_shift = jnp.sum(jnp.where(member[None, None], group_max[:, :, None, :], 0.0), axis=-1)
        soft_weights = jnp.where(listed_slot[None, None, :, None], jnp.exp(scores - slot_shift[..., None]), 0.0)
        slot_total = jnp.sum(soft_weights, axis=-1)
        soft_rounded = lax.optimization_barrier(soft_weights.astype(jnp.bfloat16)).astype(jnp.float32)
        slot_numer = jnp.einsum('hqjk,jkhd->hqjd', soft_rounded, near_values)
        member_float = member.astype(jnp.float32)
        group_total = jnp.einsum('hqj,jg->hqg', slot_total, member_float)
        group_numer = jnp.einsum('hqjd,jg->hqgd', slot_numer, member_float)
        positive = group_total > 0
        group_out = jnp.where(positive[..., None], group_numer / jnp.where(positive, group_total, 1.0)[..., None], 0.0)
        group_out = lax.optimization_barrier(group_out.astype(jnp.bfloat16)).astype(jnp.float32)
        total_rounded = lax.optimization_barrier(group_total.astype(jnp.bfloat16)).astype(jnp.float32)
        top_shift = jnp.max(group_max, axis=-1, keepdims=True)
        weight_g = total_rounded * jnp.exp(group_max - top_shift)
        attended = jnp.sum(weight_g[..., None] * group_out, axis=2) / jnp.sum(weight_g, axis=2)[..., None]
        return jnp.transpose(attended, (1, 0, 2)).reshape(BLK, attn_width).astype(jnp.bfloat16)

    attended = lax.map(one_block, (queries, neighbours, counts)).reshape(-1, attn_width)
    return jnp.dot(attended, out_weight, preferred_element_type=jnp.float32).astype(jnp.bfloat16)
```

```python
import functools

import jax
import jax.numpy as jnp
from jax import lax
from jax.experimental import pallas as pl
from jax.experimental.pallas import tpu as pltpu
from jax.sharding import Mesh, PartitionSpec as P

HD = 64
HALF = HD // 2
BLK = 128
UNROLL = 4
CHIPS_X = 4
CORES = 2
ALL = ("z", "x", "yh", "p", "c")
BF16 = jnp.bfloat16
F32 = jnp.float32


def vmem():
    return pl.BlockSpec(memory_space=pltpu.VMEM)


def smem():
    return pl.BlockSpec(memory_space=pltpu.SMEM)


def ring(size, step):
    return [(i, (i + step) % size) for i in range(size)]


def gather_weights(qkv_weight, out_weight):
    rows, width = qkv_weight.shape[0], qkv_weight.shape[1] // 3
    heads = width // HD // 2
    q_part = qkv_weight[:, :width].reshape(rows, 2, heads, 2, HALF).transpose(1, 3, 0, 2, 4)
    kv_part = qkv_weight[:, width:].reshape(rows, 2, 2, width // 2).transpose(2, 1, 0, 3)
    out_part = out_weight.T.reshape(rows, 2, 2, width // 4).transpose(1, 2, 0, 3)
    message = jnp.concatenate(
        [kv_part, q_part.reshape(2, 2, rows, width // 4), out_part], axis=-1
    )
    outer = lax.axis_size("z") * lax.axis_size("yh")
    z_size, yh_size, x_size = (lax.axis_size(name) for name in ("z", "yh", "x"))
    spread = jnp.broadcast_to(message[None], (outer,) + message.shape)
    spread = spread.reshape(outer * 4, rows, width)
    near = lax.all_to_all(spread, ("z", "yh", "p", "c"), 0, 0, tiled=True)
    near = near.reshape(1, outer * 4 * rows, width)
    near = jnp.broadcast_to(near, (x_size,) + near.shape[1:])
    return lax.all_to_all(near, "x", 0, 0, tiled=True)


def project_kernel(chunk, place, weight, own, swap_p, swap_c, swap_pc, qkv_out, out_slice, scratch):
    x_size, rows, width = weight.shape
    used = width * 3 // 4
    for z in range(rows // chunk):
        for x in range(x_size):
            at = (z * x_size + x) * chunk
            scratch[at : at + chunk, :] = weight[x, z * chunk : (z + 1) * chunk, :used]
            out_slice[at : at + chunk, :] = weight[x, z * chunk : (z + 1) * chunk, used:]
    p, c = place[0], place[1]
    blocks = ((own, p, c), (swap_p, 1 - p, c), (swap_c, p, 1 - c), (swap_pc, 1 - p, 1 - c))
    heads = used // (HD + HALF)
    for block, at_p, at_c in blocks:
        result = jnp.dot(block[...], scratch[...], preferred_element_type=F32)
        flipped = result.T.astype(BF16)
        lanes = pl.ds(pl.multiple_of((at_c * 2 + at_p) * BLK, BLK), BLK)
        for head in range(heads):
            qkv_out[head, :HD, lanes] = flipped[head * HD : (head + 1) * HD]
            at = heads * HD + head * HALF
            qkv_out[head, HD:, lanes] = flipped[at : at + HALF]


def attend_kernel(scale, place, units, lanes, counts, mine, other, out, scores):
    q_blocks = out.shape[0]
    core = place[1]

    def attend(keys, values, low, high):
        def one_block(block, carry):
            yh, p = block // 2, block % 2
            q_unit = units[q_blocks, yh]
            q_lanes = pl.ds(pl.multiple_of((core * 2 + p) * BLK, BLK), BLK)
            query = jnp.concatenate([low[q_unit, :, q_lanes], high[q_unit, :, q_lanes]], axis=0).T
            count = counts[block]
            steps = (count + UNROLL - 1) // UNROLL

            def tile(ref, slot):
                at = pl.ds(pl.multiple_of(lanes[block, slot], BLK), BLK)
                return ref[pl.ds(units[block, slot], 2), :, at].reshape(HD, BLK)

            def score(step, top):
                first = step * UNROLL
                near = jnp.concatenate([tile(keys, first + i) for i in range(UNROLL)], axis=1)
                got = jnp.dot(query, near, preferred_element_type=F32)
                for i in range(UNROLL):
                    part = got[:, i * BLK : (i + 1) * BLK]
                    part = jnp.where(first + i < count, part, -1e30)
                    scores[first + i] = part
                    top = jnp.maximum(top, part)
                return top

            top = lax.fori_loop(0, steps, score, jnp.full((BLK, BLK), -1e30, F32))
            top = jnp.max(top, axis=1, keepdims=True)

            def weigh(step, state):
                total, summed = state
                first = step * UNROLL
                soft = []
                for i in range(UNROLL):
                    part = jnp.exp((scores[first + i] - top) * scale)
                    total = total + part
                    soft.append(part.astype(BF16))
                near = jnp.concatenate([tile(values, first + i) for i in range(UNROLL)], axis=1)
                summed = summed + lax.dot_general(
                    jnp.concatenate(soft, axis=1), near, (((1,), (1,)), ((), ())),
                    preferred_element_type=F32,
                )
                return total, summed

            total, summed = lax.fori_loop(
                0, steps, weigh, (jnp.zeros((BLK, BLK), F32), jnp.zeros((BLK, HD), F32))
            )
            total = jnp.sum(total, axis=1, keepdims=True)
            out[block] = (summed / total).T.astype(BF16)
            return carry

        lax.fori_loop(0, q_blocks, one_block, 0)

    @pl.when(core == 0)
    def _():
        attend(mine, other, mine, other)

    @pl.when(core == 1)
    def _():
        attend(other, mine, other, mine)


def mix_kernel(place, attended, own, swap_c, swap_p, mixed):
    p, c = place[0], place[1]
    total = None
    for weight, at_p, at_c in (
        (own[...], p, c),
        (swap_c[...], p, 1 - c),
        (swap_p[0], 1 - p, c),
        (swap_p[1], 1 - p, 1 - c),
    ):
        pair = [attended[(at_c * 2 + i) * 2 + at_p] for i in range(2)]
        part = lax.dot_general(
            jnp.concatenate(pair, axis=0).T, weight, (((1,), (1,)), ((), ())),
            preferred_element_type=F32,
        )
        total = part if total is None else total + part
    mixed[...] = total.astype(BF16)


def body(features, order, neighbours, counts, qkv_weight, out_weight):
    dev_rows, depth = features.shape
    width = qkv_weight.shape[1] // 3
    z_size, x_size, yh_size = (lax.axis_size(name) for name in ("z", "x", "yh"))
    slabs = z_size * x_size
    ka_size = yh_size * 4
    p, c = lax.axis_index("p"), lax.axis_index("c")
    place = jnp.stack([p, c]).astype(jnp.int32)

    with jax.named_scope("weights"):
        weight = gather_weights(qkv_weight, out_weight)

    with jax.named_scope("rows"):
        own = jnp.take(features, order, axis=0)
        swap_p = lax.ppermute(own, "p", ring(2, 1))
        both = lax.ppermute(jnp.stack([own, swap_p]), "c", ring(2, 1))

    with jax.named_scope("lists"):
        slab = lax.axis_index("z") * x_size + lax.axis_index("x")
        listed = neighbours.reshape(yh_size * 2, 2, -1)
        listed = lax.dynamic_index_in_dim(listed, c, axis=1, keepdims=False)
        used = lax.dynamic_index_in_dim(counts.reshape(yh_size * 2, 2), c, axis=1, keepdims=False)
        side = (listed // ka_size - slab + 1 + slabs) % slabs
        along = listed % ka_size
        at_yh, at_p, at_c = along // 4, along // 2 % 2, along % 2
        unit = jnp.where(side == 1, yh_size * 4 + at_yh * 3, (side // 2) * yh_size * 2 + at_yh * 2)
        lane = (at_c * 2 + at_p) * BLK
        is_used = jnp.arange(listed.shape[1])[None, :] < used[:, None]
        unit = jnp.where(is_used, unit, 0)
        lane = jnp.where(is_used, lane, 0)
        q_unit = yh_size * 4 + jnp.arange(listed.shape[1]) % yh_size * 3 + 2
        unit = jnp.concatenate([unit, q_unit[None]], axis=0).astype(jnp.int32)

    chunk = weight.shape[1] // z_size
    with jax.named_scope("project"):
        qkv, out_slice = pl.pallas_call(
            functools.partial(project_kernel, chunk),
            out_shape=(
                jax.ShapeDtypeStruct((yh_size, HD + HALF, 4 * dev_rows), BF16),
                jax.ShapeDtypeStruct((depth, width // 4), BF16),
            ),
            in_specs=[smem()] + [vmem()] * 5,
            out_specs=(vmem(), vmem()),
            scratch_shapes=[pltpu.VMEM((depth, width * 3 // 4), BF16)],
            name="project",
        )(place, weight, own, swap_p, both[0], both[1])

    with jax.named_scope("heads"):
        qkv = lax.all_to_all(qkv, "yh", 0, 0, tiled=True)

    with jax.named_scope("halo"):
        key_or_value = qkv[:, :HD]
        before = lax.ppermute(key_or_value, ("z", "x"), ring(slabs, 1))
        after = lax.ppermute(key_or_value, ("z", "x"), ring(slabs, -1))
        mine = jnp.concatenate(
            [piece.reshape(-1, HALF, 4 * dev_rows) for piece in (before, after, qkv)], axis=0
        )
        other = lax.ppermute(mine, "c", ring(2, 1))

    with jax.named_scope("out_weight"):
        out_c = lax.ppermute(out_slice, "c", ring(2, 1))
        out_p = lax.ppermute(jnp.stack([out_slice, out_c]), "p", ring(2, 1))

    with jax.named_scope("attend"):
        slots = -(-neighbours.shape[1] // UNROLL) * UNROLL
        attended = pl.pallas_call(
            functools.partial(attend_kernel, HD ** -0.5),
            out_shape=jax.ShapeDtypeStruct((yh_size * 2, HD, dev_rows), BF16),
            in_specs=[smem()] * 4 + [vmem()] * 2,
            out_specs=vmem(),
            scratch_shapes=[pltpu.VMEM((slots, BLK, BLK), F32)],
            name="attend",
        )(place, unit, lane.astype(jnp.int32), used, mine, other)

    with jax.named_scope("return"):
        attended = lax.all_to_all(attended, ("yh", "p"), 0, 0, tiled=True)

    with jax.named_scope("mix"):
        return pl.pallas_call(
            mix_kernel,
            out_shape=jax.ShapeDtypeStruct((dev_rows, depth), BF16),
            in_specs=[smem()] + [vmem()] * 4,
            out_specs=vmem(),
            name="mix",
        )(place, attended, out_slice, out_c, out_p)


def solution(mesh):
    pb_size, ka_size = mesh.shape["pb"], mesh.shape["ka"]
    shape = (pb_size // CHIPS_X, CHIPS_X, ka_size // CORES // 2, 2, CORES)
    fine = Mesh(mesh.devices.reshape(shape), ALL)
    return jax.shard_map(
        body,
        mesh=fine,
        in_specs=(
            P(ALL, None),
            P(ALL),
            P(("z", "x"), None),
            P(("z", "x")),
            P(ALL, None),
            P(None, ALL),
        ),
        out_specs=P(ALL, None),
        check_vma=False,
    )
```

```python
import functools

import jax
import jax.numpy as jnp
from jax import lax
from jax.experimental import pallas as pl
from jax.experimental.pallas import tpu as pltpu
from jax.sharding import Mesh, PartitionSpec as P

HD = 64
HALF = HD // 2
BLK = 128
UNROLL = 4
TOGETHER = 4
CHIPS_X = 4
CORES = 2
LOG2_E = 1.4426950408889634
ALL = ("z", "x", "yh", "p", "c")
BF16 = jnp.bfloat16
F32 = jnp.float32

UNITS = 7


def vmem():
    return pl.BlockSpec(memory_space=pltpu.VMEM)


def smem():
    return pl.BlockSpec(memory_space=pltpu.SMEM)


def limit(mib):
    return pltpu.CompilerParams(vmem_limit_bytes=mib << 20)


def ring(size, step):
    return [(i, (i + step) % size) for i in range(size)]


def message_kernel(qkv, out_t, message):
    rows, width = qkv.shape[0], qkv.shape[1] // 3
    lane = lax.broadcasted_iota(jnp.int32, (rows, BLK), 1)
    first = lane // HALF % 2 == 0
    for p in range(2):
        at = p * width // 2
        left = qkv[:, at : at + BLK].astype(F32)
        right = qkv[:, at + BLK : at + 2 * BLK].astype(F32)
        for c in range(2):
            if c == 0:
                query = jnp.where(first, left, pltpu.roll(right, HALF, 1))
            else:
                query = jnp.where(first, pltpu.roll(left, BLK - HALF, 1), right)
            from_kv = (1 + c) * width + p * width // 2
            parts = (
                qkv[:, from_kv : from_kv + width // 2],
                query.astype(BF16),
                out_t[:, c * width // 2 : (c + 1) * width // 2],
            )
            value = jnp.concatenate(parts, axis=-1)
            message[:, p * 2 + c] = jnp.broadcast_to(value[None], (message.shape[0],) + value.shape)


def project_kernel(chunk, place, weight, mine, other, qkv_out, ordered):
    x_size, rows, used = weight.shape
    for z in range(rows // chunk):
        for x in range(x_size):
            at = (z * x_size + x) * chunk
            ordered[at : at + chunk, :] = weight[x, z * chunk : (z + 1) * chunk, :]
    p, c = place[0], place[1]
    heads = used // (HD + HALF)
    depth = ordered.shape[0]
    wide = heads * HD

    def lanes(at_c, j):
        return pl.ds(pl.multiple_of((at_c * 2 + (p if j == 0 else 1 - p)) * BLK, BLK), BLK)

    for ref, at_c in ((mine, c), (other, 1 - c)):
        result = jnp.dot(
            ref[:2].reshape(2 * BLK, depth), ordered[...], preferred_element_type=F32
        )
        flipped = result.astype(BF16).T
        for j in range(2):
            part = flipped[:, j * BLK : (j + 1) * BLK]
            for head in range(heads):
                qkv_out[head, :HD, lanes(at_c, j)] = part[head * HD : (head + 1) * HD]
                at = wide + (head % 2 * 2 + head // 2) * HALF
                qkv_out[head, HD : HD + HALF, lanes(at_c, j)] = part[at : at + HALF]
    for ref, at_c in ((mine, c), (other, 1 - c)):
        result = jnp.dot(
            ref[2:].reshape(4 * BLK, depth), ordered[:, :wide], preferred_element_type=F32
        )
        flipped = result.astype(BF16).T
        for side in range(2):
            for j in range(2):
                at = (side * 2 + j) * BLK
                part = flipped[:, at : at + BLK]
                to = HD + HALF + side * HD
                for head in range(heads):
                    qkv_out[head, to : to + HD, lanes(at_c, j)] = part[head * HD : (head + 1) * HD]


def attend_kernel(scale, place, units, lanes, counts, mine, other, out, scores):
    q_blocks = out.shape[0]
    slots = scores.shape[1]
    core = place[1]

    def attend(keys, values, low, high):
        def one_block(block, room):
            yh, p = block // 2, block % 2
            q_unit = yh * UNITS + 2
            q_lanes = pl.ds(pl.multiple_of((core * 2 + p) * BLK, BLK), BLK)
            query = jnp.concatenate([low[q_unit, :, q_lanes], high[q_unit, :, q_lanes]], axis=0).T
            count = counts[block]

            def tiles(ref, first):
                found = []
                for slot in range(first, first + UNROLL):
                    at = pl.ds(pl.multiple_of(lanes[block, slot], BLK), BLK)
                    found.append(ref[pl.ds(units[block, slot], 2), :, at].reshape(HD, BLK))
                return jnp.concatenate(found, axis=1)

            top = jnp.full((BLK, BLK), -1e30, F32)
            for first in range(0, slots, UNROLL):
                got = jnp.dot(query, tiles(keys, first), preferred_element_type=F32)
                got = got * (scale * LOG2_E)
                for i in range(UNROLL):
                    part = jnp.where(first + i < count, got[:, i * BLK : (i + 1) * BLK], -1e30)
                    scores[room, first + i] = part
                    top = jnp.maximum(top, part)
            top = jnp.max(top, axis=1, keepdims=True)

            total = jnp.zeros((BLK, BLK), F32)
            summed = jnp.zeros((BLK, HD), F32)
            for first in range(0, slots, UNROLL):
                soft = []
                for i in range(UNROLL):
                    part = jnp.exp2(scores[room, first + i] - top)
                    total = total + part
                    soft.append(part.astype(BF16))
                summed = summed + lax.dot_general(
                    jnp.concatenate(soft, axis=1), tiles(values, first), (((1,), (1,)), ((), ())),
                    preferred_element_type=F32,
                )
            total = jnp.sum(total, axis=1, keepdims=True)
            out[block] = (summed / total).T.astype(BF16)

        def several(step, carry):
            for room in range(TOGETHER):
                one_block(step * TOGETHER + room, room)
            return carry

        lax.fori_loop(0, q_blocks // TOGETHER, several, 0)

    @pl.when(core == 0)
    def _():
        attend(mine, other, mine, other)

    @pl.when(core == 1)
    def _():
        attend(other, mine, other, mine)


def order_kernel(chunk, place, *refs):
    pieces, out = refs[:-1], refs[-1]
    count = len(pieces)
    for k, piece in enumerate(pieces):
        x = lax.rem(place[2] + k, count)
        for z in range(piece.shape[0] // chunk):
            at = pl.ds(pl.multiple_of((z * count + x) * chunk, chunk), chunk)
            out[at, :] = piece[z * chunk : (z + 1) * chunk, :]


def mix_kernel(place, attended, own, other, mixed):
    c = place[1]
    total = None
    for weight, at_c in ((own, c), (other, 1 - c)):
        heads = [attended[i * 2 + at_c] for i in range(attended.shape[0] // 2)]
        part = lax.dot_general(
            jnp.concatenate(heads, axis=0).T, weight[...], (((1,), (1,)), ((), ())),
            preferred_element_type=F32,
        )
        total = part if total is None else total + part
    mixed[...] = total.astype(BF16)


def block_lists(neighbours, counts, c, slab, slabs, yh_size):
    ka_size = yh_size * 4
    listed = neighbours.reshape(yh_size * 2, 2, -1)
    listed = lax.dynamic_index_in_dim(listed, c, axis=1, keepdims=False)
    used = lax.dynamic_index_in_dim(counts.reshape(yh_size * 2, 2), c, axis=1, keepdims=False)
    side = (listed // ka_size - slab + 1 + slabs) % slabs
    along = listed % ka_size
    offset = jnp.where(side == 1, 0, jnp.where(side == 0, 3, 5))
    unit = along // 4 * UNITS + offset
    lane = (along % 2 * 2 + along // 2 % 2) * BLK
    is_used = jnp.arange(listed.shape[1])[None, :] < used[:, None]
    return (
        jnp.where(is_used, unit, 0).astype(jnp.int32),
        jnp.where(is_used, lane, 0).astype(jnp.int32),
        used,
    )


def body(features, order, neighbours, counts, qkv_weight, out_weight):
    dev_rows, depth = features.shape
    rows, width = qkv_weight.shape[0], qkv_weight.shape[1] // 3
    z_size, x_size, yh_size = (lax.axis_size(name) for name in ("z", "x", "yh"))
    slabs = z_size * x_size
    p, c = lax.axis_index("p"), lax.axis_index("c")
    slab = lax.axis_index("z") * x_size + lax.axis_index("x")
    place = jnp.stack([p, c, lax.axis_index("x")]).astype(jnp.int32)
    used_width = width * 3 // 4

    with jax.named_scope("weights_near"):
        per_class = used_width + width // 2
        message = pl.pallas_call(
            message_kernel,
            out_shape=jax.ShapeDtypeStruct((z_size * yh_size, 4, rows, per_class), BF16),
            in_specs=[vmem()] * 2,
            out_specs=vmem(),
            compiler_params=limit(16),
            name="message",
        )(qkv_weight, out_weight.T)
        message = message.reshape(-1, rows, per_class)

    with jax.named_scope("rows"):
        message, order = lax.optimization_barrier((message, order))
        own = features.at[order].get(mode="promise_in_bounds")
        blocks = [own, lax.ppermute(own, "p", ring(2, 1))]
        for step in (1, -1):
            blocks.append(lax.ppermute(own, ("z", "x"), ring(slabs, step)))
            across = [(i, (i // 2 + step) % slabs * 2 + 1 - i % 2) for i in range(slabs * 2)]
            blocks.append(lax.ppermute(own, ("z", "x", "p"), across))

    with jax.named_scope("weights_near"):
        near = lax.all_to_all(message, ("z", "yh", "p", "c"), 0, 0, tiled=True)
        near = near.reshape(-1, per_class)

    with jax.named_scope("lists"):
        lists = block_lists(neighbours, counts, c, slab, slabs, yh_size)
        near, lists = lax.optimization_barrier((near, lists))
        unit, lane, used = lists

    with jax.named_scope("weights_far"):
        spread = jnp.broadcast_to(near[None, :, :used_width], (x_size, near.shape[0], used_width))
        weight = lax.all_to_all(spread, "x", 0, 0, tiled=True)
        _, blocks = lax.optimization_barrier((spread, blocks))
        blocks = jnp.stack(blocks)
        blocks_other = lax.ppermute(blocks, "c", ring(2, 1))

    with jax.named_scope("project"):
        qkv = pl.pallas_call(
            functools.partial(project_kernel, near.shape[0] // z_size),
            out_shape=jax.ShapeDtypeStruct((yh_size, UNITS * HALF, 4 * dev_rows), BF16),
            in_specs=[smem()] + [vmem()] * 3,
            out_specs=vmem(),
            scratch_shapes=[pltpu.VMEM((depth, used_width), BF16)],
            compiler_params=limit(24),
            name="project",
        )(place, weight, blocks, blocks_other)
        qkv, near_out = lax.optimization_barrier((qkv, near[:, used_width:]))

    with jax.named_scope("heads"):
        mine = lax.all_to_all(qkv, "yh", 0, 0, tiled=True)

    with jax.named_scope("out_weight"):
        pieces = [near_out] + [lax.ppermute(near_out, "x", ring(x_size, -k)) for k in range(1, x_size)]
        out_own = pl.pallas_call(
            functools.partial(order_kernel, near.shape[0] // z_size),
            out_shape=jax.ShapeDtypeStruct((depth, width // 2), BF16),
            in_specs=[smem()] + [vmem()] * x_size,
            out_specs=vmem(),
            compiler_params=limit(16),
            name="order",
        )(place, *pieces)
        out_other = lax.ppermute(out_own, "c", ring(2, 1))
        mine, out_own, out_other = lax.optimization_barrier((mine, out_own, out_other))
        mine = mine.reshape(-1, HALF, 4 * dev_rows)

    with jax.named_scope("attend"):
        other = lax.ppermute(mine, "c", ring(2, 1))
        slots = -(-neighbours.shape[1] // UNROLL) * UNROLL
        attended = pl.pallas_call(
            functools.partial(attend_kernel, HD ** -0.5),
            out_shape=jax.ShapeDtypeStruct((yh_size * 2, HD, dev_rows), BF16),
            in_specs=[smem()] * 4 + [vmem()] * 2,
            out_specs=vmem(),
            scratch_shapes=[pltpu.VMEM((TOGETHER, slots, BLK, BLK), F32)],
            compiler_params=limit(24),
            name="attend",
        )(place, unit, lane, used, mine, other)

    with jax.named_scope("return"):
        attended = lax.all_to_all(attended, ("yh", "p"), 0, 0, tiled=True)

    with jax.named_scope("mix"):
        return pl.pallas_call(
            mix_kernel,
            out_shape=jax.ShapeDtypeStruct((dev_rows, depth), BF16),
            in_specs=[smem()] + [vmem()] * 3,
            out_specs=vmem(),
            compiler_params=limit(16),
            name="mix",
        )(place, attended, out_own, out_other)


def solution(mesh):
    pb_size, ka_size = mesh.shape["pb"], mesh.shape["ka"]
    shape = (pb_size // CHIPS_X, CHIPS_X, ka_size // CORES // 2, 2, CORES)
    fine = Mesh(mesh.devices.reshape(shape), ALL)
    return jax.shard_map(
        body,
        mesh=fine,
        in_specs=(
            P(ALL, None),
            P(ALL),
            P(("z", "x"), None),
            P(("z", "x")),
            P(ALL, None),
            P(None, ALL),
        ),
        out_specs=P(ALL, None),
        check_vma=False,
    )
```

```python
import functools

import jax
import jax.numpy as jnp
from jax import lax
from jax.experimental import pallas as pl
from jax.experimental.pallas import tpu as pltpu
from jax.sharding import Mesh, PartitionSpec as P

HD = 64
HALF = HD // 2
BLK = 128
UNROLL = 4
TOGETHER = 4
CHIPS_X = 4
CORES = 2
LOG2_E = 1.4426950408889634
ALL = ("z", "x", "yh", "p", "c")
BF16 = jnp.bfloat16
F32 = jnp.float32

UNITS = 7


def vmem():
    return pl.BlockSpec(memory_space=pltpu.VMEM)


def smem():
    return pl.BlockSpec(memory_space=pltpu.SMEM)


def limit(mib):
    return pltpu.CompilerParams(vmem_limit_bytes=mib << 20)


def ring(size, step):
    return [(i, (i + step) % size) for i in range(size)]


def message_kernel(order, features, qkv, out_t, message, own):
    position = lax.broadcasted_iota(jnp.int32, (order.shape[1],) * 2, 0)
    picks = jnp.where(position == order[...], 1.0, 0.0).T.astype(BF16)
    own[...] = jnp.dot(picks, features[...], preferred_element_type=F32).astype(BF16)
    rows, width = qkv.shape[0], qkv.shape[1] // 3
    lane = lax.broadcasted_iota(jnp.int32, (rows, BLK), 1)
    first = lane // HALF % 2 == 0
    for p in range(2):
        at = p * width // 2
        left = qkv[:, at : at + BLK].astype(F32)
        right = qkv[:, at + BLK : at + 2 * BLK].astype(F32)
        for c in range(2):
            if c == 0:
                query = jnp.where(first, left, pltpu.roll(right, HALF, 1))
            else:
                query = jnp.where(first, pltpu.roll(left, BLK - HALF, 1), right)
            from_kv = (1 + c) * width + p * width // 2
            parts = (
                qkv[:, from_kv : from_kv + width // 2],
                query.astype(BF16),
                out_t[:, c * width // 2 : (c + 1) * width // 2],
            )
            value = jnp.concatenate(parts, axis=-1)
            message[:, p * 2 + c] = jnp.broadcast_to(value[None], (message.shape[0],) + value.shape)


def project_kernel(chunk, place, weight, *refs):
    mine, other, (qkv_out, ordered) = refs[:3], refs[3:6], refs[6:]
    x_size, rows, used = weight.shape
    for z in range(rows // chunk):
        for x in range(x_size):
            at = (z * x_size + x) * chunk
            ordered[at : at + chunk, :] = weight[x, z * chunk : (z + 1) * chunk, :]
    p, c = place[0], place[1]
    heads = used // (HD + HALF)
    depth = ordered.shape[0]
    wide = heads * HD

    for blocks, at_c in ((mine, c), (other, 1 - c)):
        for side, pair in enumerate(blocks):
            columns = used if side == 0 else wide
            to = 0 if side == 0 else HALF + side * HD
            result = jnp.dot(
                pair[...].reshape(2 * BLK, depth), ordered[:, :columns], preferred_element_type=F32
            )
            flipped = result.astype(BF16).T
            for j in range(2):
                at_p = p if j == 0 else 1 - p
                lanes = pl.ds(pl.multiple_of((at_c * 2 + at_p) * BLK, BLK), BLK)
                part = flipped[:, j * BLK : (j + 1) * BLK]
                for head in range(heads):
                    qkv_out[head, to : to + HD, lanes] = part[head * HD : (head + 1) * HD]
                    if side == 0:
                        at = wide + (head % 2 * 2 + head // 2) * HALF
                        qkv_out[head, HD : HD + HALF, lanes] = part[at : at + HALF]


def attend_kernel(scale, place, units, lanes, counts, mine, other, out, scores):
    q_blocks = out.shape[0]
    slots = scores.shape[1]
    core = place[1]

    def attend(keys, values, low, high):
        def one_block(block, room):
            yh, p = block // 2, block % 2
            q_unit = yh * UNITS + 2
            q_lanes = pl.ds(pl.multiple_of((core * 2 + p) * BLK, BLK), BLK)
            query = jnp.concatenate([low[q_unit, :, q_lanes], high[q_unit, :, q_lanes]], axis=0).T
            count = counts[block]

            def tiles(ref, first):
                found = []
                for slot in range(first, first + UNROLL):
                    at = pl.ds(pl.multiple_of(lanes[block, slot], BLK), BLK)
                    found.append(ref[pl.ds(units[block, slot], 2), :, at].reshape(HD, BLK))
                return jnp.concatenate(found, axis=1)

            top = jnp.full((BLK, BLK), -1e30, F32)
            for first in range(0, slots, UNROLL):
                got = jnp.dot(query, tiles(keys, first), preferred_element_type=F32)
                got = got * (scale * LOG2_E)
                for i in range(UNROLL):
                    part = jnp.where(first + i < count, got[:, i * BLK : (i + 1) * BLK], -1e30)
                    scores[room, first + i] = part
                    top = jnp.maximum(top, part)
            top = jnp.max(top, axis=1, keepdims=True)

            total = jnp.zeros((BLK, BLK), F32)
            summed = jnp.zeros((BLK, HD), F32)
            for first in range(0, slots, UNROLL):
                soft = []
                for i in range(UNROLL):
                    part = jnp.exp2(scores[room, first + i] - top)
                    total = total + part
                    soft.append(part.astype(BF16))
                summed = summed + lax.dot_general(
                    jnp.concatenate(soft, axis=1), tiles(values, first), (((1,), (1,)), ((), ())),
                    preferred_element_type=F32,
                )
            total = jnp.sum(total, axis=1, keepdims=True)
            out[block] = (summed / total).T.astype(BF16)

        def several(step, carry):
            for room in range(TOGETHER):
                one_block(step * TOGETHER + room, room)
            return carry

        lax.fori_loop(0, q_blocks // TOGETHER, several, 0)

    @pl.when(core == 0)
    def _():
        attend(mine, other, mine, other)

    @pl.when(core == 1)
    def _():
        attend(other, mine, other, mine)


def order_kernel(chunk, place, *refs):
    pieces, out = refs[:-1], refs[-1]
    count = len(pieces)
    for k, piece in enumerate(pieces):
        x = lax.rem(place[2] + k, count)
        for z in range(piece.shape[0] // chunk):
            at = pl.ds(pl.multiple_of((z * count + x) * chunk, chunk), chunk)
            out[at, :] = piece[z * chunk : (z + 1) * chunk, :]


def mix_kernel(place, attended, own, other, mixed):
    c = place[1]
    total = None
    for weight, at_c in ((own, c), (other, 1 - c)):
        heads = [attended[i * 2 + at_c] for i in range(attended.shape[0] // 2)]
        part = lax.dot_general(
            jnp.concatenate(heads, axis=0).T, weight[...], (((1,), (1,)), ((), ())),
            preferred_element_type=F32,
        )
        total = part if total is None else total + part
    mixed[...] = total.astype(BF16)


def block_lists(neighbours, counts, c, slab, slabs, yh_size):
    ka_size = yh_size * 4
    listed = neighbours.reshape(yh_size * 2, 2, -1)
    listed = lax.dynamic_index_in_dim(listed, c, axis=1, keepdims=False)
    used = lax.dynamic_index_in_dim(counts.reshape(yh_size * 2, 2), c, axis=1, keepdims=False)
    side = (listed // ka_size - slab + 1 + slabs) % slabs
    along = listed % ka_size
    offset = jnp.where(side == 1, 0, jnp.where(side == 0, 3, 5))
    unit = along // 4 * UNITS + offset
    lane = (along % 2 * 2 + along // 2 % 2) * BLK
    is_used = jnp.arange(listed.shape[1])[None, :] < used[:, None]
    return (
        jnp.where(is_used, unit, 0).astype(jnp.int32),
        jnp.where(is_used, lane, 0).astype(jnp.int32),
        used,
    )


def body(features, order, neighbours, counts, qkv_weight, out_weight):
    dev_rows, depth = features.shape
    rows, width = qkv_weight.shape[0], qkv_weight.shape[1] // 3
    z_size, x_size, yh_size = (lax.axis_size(name) for name in ("z", "x", "yh"))
    slabs = z_size * x_size
    p, c = lax.axis_index("p"), lax.axis_index("c")
    slab = lax.axis_index("z") * x_size + lax.axis_index("x")
    place = jnp.stack([p, c, lax.axis_index("x")]).astype(jnp.int32)
    used_width = width * 3 // 4

    with jax.named_scope("weights_near"):
        per_class = used_width + width // 2
        message, own = pl.pallas_call(
            message_kernel,
            out_shape=(
                jax.ShapeDtypeStruct((z_size * yh_size, 4, rows, per_class), BF16),
                jax.ShapeDtypeStruct(features.shape, BF16),
            ),
            in_specs=[vmem()] * 4,
            out_specs=(vmem(), vmem()),
            compiler_params=limit(16),
            name="message",
        )(order.reshape(1, -1), features, qkv_weight, out_weight.T)
        message = message.reshape(-1, rows, per_class)

    with jax.named_scope("rows"):
        pair = jnp.stack([own, lax.ppermute(own, "p", ring(2, 1))])
        before = lax.ppermute(pair, ("z", "x"), ring(slabs, 1))
        after = lax.ppermute(pair, ("z", "x"), ring(slabs, -1))

    with jax.named_scope("weights_near"):
        near = lax.all_to_all(message, ("z", "yh", "p", "c"), 0, 0, tiled=True)
        near = near.reshape(-1, per_class)

    with jax.named_scope("lists"):
        lists = block_lists(neighbours, counts, c, slab, slabs, yh_size)
        near, lists = lax.optimization_barrier((near, lists))
        unit, lane, used = lists

    with jax.named_scope("weights_far"):
        spread = jnp.broadcast_to(near[None, :, :used_width], (x_size, near.shape[0], used_width))
        weight = lax.all_to_all(spread, "x", 0, 0, tiled=True)
        _, mine = lax.optimization_barrier((spread, (pair, before, after)))
        other = [lax.ppermute(piece, "c", ring(2, 1)) for piece in mine]

    with jax.named_scope("project"):
        qkv = pl.pallas_call(
            functools.partial(project_kernel, near.shape[0] // z_size),
            out_shape=jax.ShapeDtypeStruct((yh_size, UNITS * HALF, 4 * dev_rows), BF16),
            in_specs=[smem()] + [vmem()] * 7,
            out_specs=vmem(),
            scratch_shapes=[pltpu.VMEM((depth, used_width), BF16)],
            compiler_params=limit(24),
            name="project",
        )(place, weight, *mine, *other)
        qkv, near_out = lax.optimization_barrier((qkv, near[:, used_width:]))

    with jax.named_scope("heads"):
        mine = lax.all_to_all(qkv, "yh", 0, 0, tiled=True)

    with jax.named_scope("out_weight"):
        pieces = [near_out] + [lax.ppermute(near_out, "x", ring(x_size, -k)) for k in range(1, x_size)]
        out_own = pl.pallas_call(
            functools.partial(order_kernel, near.shape[0] // z_size),
            out_shape=jax.ShapeDtypeStruct((depth, width // 2), BF16),
            in_specs=[smem()] + [vmem()] * x_size,
            out_specs=vmem(),
            compiler_params=limit(16),
            name="order",
        )(place, *pieces)
        out_other = lax.ppermute(out_own, "c", ring(2, 1))
        mine, out_own, out_other = lax.optimization_barrier((mine, out_own, out_other))
        mine = mine.reshape(-1, HALF, 4 * dev_rows)

    with jax.named_scope("attend"):
        other = lax.ppermute(mine, "c", ring(2, 1))
        slots = -(-neighbours.shape[1] // UNROLL) * UNROLL
        attended = pl.pallas_call(
            functools.partial(attend_kernel, HD ** -0.5),
            out_shape=jax.ShapeDtypeStruct((yh_size * 2, HD, dev_rows), BF16),
            in_specs=[smem()] * 4 + [vmem()] * 2,
            out_specs=vmem(),
            scratch_shapes=[pltpu.VMEM((TOGETHER, slots, BLK, BLK), F32)],
            compiler_params=limit(24),
            name="attend",
        )(place, unit, lane, used, mine, other)

    with jax.named_scope("return"):
        attended = lax.all_to_all(attended, ("yh", "p"), 0, 0, tiled=True)

    with jax.named_scope("mix"):
        return pl.pallas_call(
            mix_kernel,
            out_shape=jax.ShapeDtypeStruct((dev_rows, depth), BF16),
            in_specs=[smem()] + [vmem()] * 3,
            out_specs=vmem(),
            compiler_params=limit(16),
            name="mix",
        )(place, attended, out_own, out_other)


def solution(mesh):
    pb_size, ka_size = mesh.shape["pb"], mesh.shape["ka"]
    shape = (pb_size // CHIPS_X, CHIPS_X, ka_size // CORES // 2, 2, CORES)
    fine = Mesh(mesh.devices.reshape(shape), ALL)
    return jax.shard_map(
        body,
        mesh=fine,
        in_specs=(
            P(ALL, None),
            P(ALL),
            P(("z", "x"), None),
            P(("z", "x")),
            P(ALL, None),
            P(None, ALL),
        ),
        out_specs=P(ALL, None),
        check_vma=False,
    )
```

```python
import functools

import jax
import jax.numpy as jnp
from jax import lax
from jax.experimental import pallas as pl
from jax.experimental.pallas import tpu as pltpu
from jax.sharding import Mesh, PartitionSpec as P

HD = 64
HALF = HD // 2
BLK = 128
UNROLL = 4
TOGETHER = 8
CHIPS_X = 4
CORES = 2
LOG2_E = 1.4426950408889634
ALL = ("z", "x", "yh", "p", "c")
BF16 = jnp.bfloat16
F32 = jnp.float32

UNITS = 7


def vmem():
    return pl.BlockSpec(memory_space=pltpu.VMEM)


def smem():
    return pl.BlockSpec(memory_space=pltpu.SMEM)


def limit(mib):
    return pltpu.CompilerParams(vmem_limit_bytes=mib << 20)


def ring(size, step):
    return [(i, (i + step) % size) for i in range(size)]


def message_kernel(order, features, qkv, out_t, message, own):
    position = lax.broadcasted_iota(jnp.int32, (order.shape[1],) * 2, 0)
    picks = jnp.where(position == order[...], 1.0, 0.0).T.astype(BF16)
    own[...] = jnp.dot(picks, features[...], preferred_element_type=F32).astype(BF16)
    rows, width = qkv.shape[0], qkv.shape[1] // 3
    lane = lax.broadcasted_iota(jnp.int32, (rows, BLK), 1)
    first = lane // HALF % 2 == 0
    for p in range(2):
        at = p * width // 2
        left = qkv[:, at : at + BLK].astype(F32)
        right = qkv[:, at + BLK : at + 2 * BLK].astype(F32)
        for c in range(2):
            if c == 0:
                query = jnp.where(first, left, pltpu.roll(right, HALF, 1))
            else:
                query = jnp.where(first, pltpu.roll(left, BLK - HALF, 1), right)
            from_kv = (1 + c) * width + p * width // 2
            parts = (
                qkv[:, from_kv : from_kv + width // 2],
                query.astype(BF16),
                out_t[:, c * width // 2 : (c + 1) * width // 2],
            )
            value = jnp.concatenate(parts, axis=-1)
            message[:, p * 2 + c] = jnp.broadcast_to(value[None], (message.shape[0],) + value.shape)


def project_kernel(chunk, weight, *refs):
    mine, other, (qkv_out, ordered) = refs[:3], refs[3:6], refs[6:]
    x_size, rows, used = weight.shape
    for z in range(rows // chunk):
        for x in range(x_size):
            at = (z * x_size + x) * chunk
            ordered[at : at + chunk, :] = weight[x, z * chunk : (z + 1) * chunk, :]
    p, c = lax.axis_index("p"), lax.axis_index("c")
    heads = used // (HD + HALF)
    depth = ordered.shape[0]
    wide = heads * HD

    for blocks, at_c in ((mine, c), (other, 1 - c)):
        for side, pair in enumerate(blocks):
            columns = used if side == 0 else wide
            to = 0 if side == 0 else HALF + side * HD
            result = jnp.dot(
                pair[...].reshape(2 * BLK, depth), ordered[:, :columns], preferred_element_type=F32
            )
            flipped = result.astype(BF16).T
            for j in range(2):
                at_p = p if j == 0 else 1 - p
                lanes = pl.ds(pl.multiple_of((at_c * 2 + at_p) * BLK, BLK), BLK)
                part = flipped[:, j * BLK : (j + 1) * BLK]
                for head in range(heads):
                    qkv_out[head, to : to + HD, lanes] = part[head * HD : (head + 1) * HD]
                    if side == 0:
                        at = wide + (head % 2 * 2 + head // 2) * HALF
                        qkv_out[head, HD : HD + HALF, lanes] = part[at : at + HALF]


def attend_kernel(scale, units, lanes, counts, mine, other, out, scores):
    q_blocks = out.shape[0]
    slots = scores.shape[1]
    core = lax.axis_index("c")

    def attend(keys, values, low, high):
        def one_block(block, room):
            yh, p = block // 2, block % 2
            q_unit = yh * UNITS + 2
            q_lanes = pl.ds(pl.multiple_of((core * 2 + p) * BLK, BLK), BLK)
            query = jnp.concatenate([low[q_unit, :, q_lanes], high[q_unit, :, q_lanes]], axis=0).T
            count = counts[block]

            def tiles(ref, first):
                found = []
                for slot in range(first, first + UNROLL):
                    at = pl.ds(pl.multiple_of(lanes[block, slot], BLK), BLK)
                    found.append(ref[pl.ds(units[block, slot], 2), :, at].reshape(HD, BLK))
                return jnp.concatenate(found, axis=1)

            top = jnp.full((BLK, BLK), -1e30, F32)
            for first in range(0, slots, UNROLL):
                got = jnp.dot(query, tiles(keys, first), preferred_element_type=F32)
                got = got * (scale * LOG2_E)
                for i in range(UNROLL):
                    part = jnp.where(first + i < count, got[:, i * BLK : (i + 1) * BLK], -1e30)
                    scores[room, first + i] = part
                    top = jnp.maximum(top, part)
            top = jnp.max(top, axis=1, keepdims=True)

            total = jnp.zeros((BLK, BLK), F32)
            summed = jnp.zeros((BLK, HD), F32)
            for first in range(0, slots, UNROLL):
                soft = []
                for i in range(UNROLL):
                    part = jnp.exp2(scores[room, first + i] - top)
                    total = total + part
                    soft.append(part.astype(BF16))
                summed = summed + lax.dot_general(
                    jnp.concatenate(soft, axis=1), tiles(values, first), (((1,), (1,)), ((), ())),
                    preferred_element_type=F32,
                )
            total = jnp.sum(total, axis=1, keepdims=True)
            out[block] = (summed / total).T.astype(BF16)

        def several(step, carry):
            for room in range(TOGETHER):
                one_block(step * TOGETHER + room, room)
            return carry

        lax.fori_loop(0, q_blocks // TOGETHER, several, 0)

    @pl.when(core == 0)
    def _():
        attend(mine, other, mine, other)

    @pl.when(core == 1)
    def _():
        attend(other, mine, other, mine)


def order_kernel(chunk, *refs):
    pieces, out = refs[:-1], refs[-1]
    count = len(pieces)
    for k, piece in enumerate(pieces):
        x = lax.rem(lax.axis_index("x") + k, count)
        for z in range(piece.shape[0] // chunk):
            at = pl.ds(pl.multiple_of((z * count + x) * chunk, chunk), chunk)
            out[at, :] = piece[z * chunk : (z + 1) * chunk, :]


def mix_kernel(attended, own, other, mixed):
    c = lax.axis_index("c")
    total = None
    for weight, at_c in ((own, c), (other, 1 - c)):
        heads = [attended[i * 2 + at_c] for i in range(attended.shape[0] // 2)]
        part = lax.dot_general(
            jnp.concatenate(heads, axis=0).T, weight[...], (((1,), (1,)), ((), ())),
            preferred_element_type=F32,
        )
        total = part if total is None else total + part
    mixed[...] = total.astype(BF16)


def block_lists(neighbours, counts, c, slab, slabs, yh_size):
    ka_size = yh_size * 4
    listed = neighbours.reshape(yh_size * 2, 2, -1)
    listed = lax.dynamic_index_in_dim(listed, c, axis=1, keepdims=False)
    used = lax.dynamic_index_in_dim(counts.reshape(yh_size * 2, 2), c, axis=1, keepdims=False)
    side = (listed // ka_size - slab + 1 + slabs) % slabs
    along = listed % ka_size
    offset = jnp.where(side == 1, 0, jnp.where(side == 0, 3, 5))
    unit = along // 4 * UNITS + offset
    lane = (along % 2 * 2 + along // 2 % 2) * BLK
    is_used = jnp.arange(listed.shape[1])[None, :] < used[:, None]
    return (
        jnp.where(is_used, unit, 0).astype(jnp.int32),
        jnp.where(is_used, lane, 0).astype(jnp.int32),
        used,
    )


def body(features, order, neighbours, counts, qkv_weight, out_weight):
    dev_rows, depth = features.shape
    rows, width = qkv_weight.shape[0], qkv_weight.shape[1] // 3
    z_size, x_size, yh_size = (lax.axis_size(name) for name in ("z", "x", "yh"))
    slabs = z_size * x_size
    c = lax.axis_index("c")
    slab = lax.axis_index("z") * x_size + lax.axis_index("x")
    used_width = width * 3 // 4

    with jax.named_scope("weights_near"):
        per_class = used_width + width // 2
        message, own = pl.pallas_call(
            message_kernel,
            out_shape=(
                jax.ShapeDtypeStruct((z_size * yh_size, 4, rows, per_class), BF16),
                jax.ShapeDtypeStruct(features.shape, BF16),
            ),
            in_specs=[vmem()] * 4,
            out_specs=(vmem(), vmem()),
            name="message",
        )(order.reshape(1, -1), features, qkv_weight, out_weight.T)
        message = message.reshape(-1, rows, per_class)

    with jax.named_scope("rows"):
        pair = jnp.stack([own, lax.ppermute(own, "p", ring(2, 1))])
        before = lax.ppermute(pair, ("z", "x"), ring(slabs, 1))
        after = lax.ppermute(pair, ("z", "x"), ring(slabs, -1))

    with jax.named_scope("weights_near"):
        near = lax.all_to_all(message, ("z", "yh", "p", "c"), 0, 0, tiled=True)
        near = near.reshape(-1, per_class)

    with jax.named_scope("lists"):
        lists = block_lists(neighbours, counts, c, slab, slabs, yh_size)
        near, lists = lax.optimization_barrier((near, lists))
        unit, lane, used = lists

    with jax.named_scope("weights_far"):
        spread = jnp.broadcast_to(near[None, :, :used_width], (x_size, near.shape[0], used_width))
        weight = lax.all_to_all(spread, "x", 0, 0, tiled=True)
        _, mine = lax.optimization_barrier((spread, (pair, before, after)))
        other = [lax.ppermute(piece, "c", ring(2, 1)) for piece in mine]

    with jax.named_scope("project"):
        qkv = pl.pallas_call(
            functools.partial(project_kernel, near.shape[0] // z_size),
            out_shape=jax.ShapeDtypeStruct((yh_size, UNITS * HALF, 4 * dev_rows), BF16),
            in_specs=[vmem()] * 7,
            out_specs=vmem(),
            scratch_shapes=[pltpu.VMEM((depth, used_width), BF16)],
            compiler_params=limit(24),
            name="project",
        )(weight, *mine, *other)
        qkv, near = lax.optimization_barrier((qkv, near))
        near_out = near[:, used_width:]

    with jax.named_scope("heads"):
        mine = lax.all_to_all(qkv, "yh", 0, 0, tiled=True)

    with jax.named_scope("out_weight"):
        pieces = [near_out] + [lax.ppermute(near_out, "x", ring(x_size, -k)) for k in range(1, x_size)]
        out_own = pl.pallas_call(
            functools.partial(order_kernel, near.shape[0] // z_size),
            out_shape=jax.ShapeDtypeStruct((depth, width // 2), BF16),
            in_specs=[vmem()] * x_size,
            out_specs=vmem(),
            compiler_params=limit(16),
            name="order",
        )(*pieces)
        out_other = lax.ppermute(out_own, "c", ring(2, 1))
        mine, out_own, out_other = lax.optimization_barrier((mine, out_own, out_other))
        mine = mine.reshape(-1, HALF, 4 * dev_rows)

    with jax.named_scope("attend"):
        other = lax.ppermute(mine, "c", ring(2, 1))
        slots = -(-neighbours.shape[1] // UNROLL) * UNROLL
        attended = pl.pallas_call(
            functools.partial(attend_kernel, HD ** -0.5),
            out_shape=jax.ShapeDtypeStruct((yh_size * 2, HD, dev_rows), BF16),
            in_specs=[smem()] * 3 + [vmem()] * 2,
            out_specs=vmem(),
            scratch_shapes=[pltpu.VMEM((TOGETHER, slots, BLK, BLK), F32)],
            compiler_params=limit(24),
            name="attend",
        )(unit, lane, used, mine, other)

    with jax.named_scope("return"):
        attended = lax.all_to_all(attended, ("yh", "p"), 0, 0, tiled=True)

    with jax.named_scope("mix"):
        return pl.pallas_call(
            mix_kernel,
            out_shape=jax.ShapeDtypeStruct((dev_rows, depth), BF16),
            in_specs=[vmem()] * 3,
            out_specs=vmem(),
            compiler_params=limit(16),
            name="mix",
        )(attended, out_own, out_other)


def solution(mesh):
    pb_size, ka_size = mesh.shape["pb"], mesh.shape["ka"]
    shape = (pb_size // CHIPS_X, CHIPS_X, ka_size // CORES // 2, 2, CORES)
    fine = Mesh(mesh.devices.reshape(shape), ALL)
    return jax.shard_map(
        body,
        mesh=fine,
        in_specs=(
            P(ALL, None),
            P(ALL),
            P(("z", "x"), None),
            P(("z", "x")),
            P(ALL, None),
            P(None, ALL),
        ),
        out_specs=P(ALL, None),
        check_vma=False,
    )
```

```python
import functools

import jax
import jax.numpy as jnp
from jax import lax
from jax.experimental import pallas as pl
from jax.experimental.pallas import tpu as pltpu
from jax.sharding import Mesh, PartitionSpec as P

HD = 64
HALF = HD // 2
BLK = 128
UNROLL = 4
TOGETHER = 8
CHIPS_X = 4
CORES = 2
LOG2_E = 1.4426950408889634
ALL = ("z", "x", "yh", "p", "c")
BF16 = jnp.bfloat16
F32 = jnp.float32

UNITS = 7


def vmem():
    return pl.BlockSpec(memory_space=pltpu.VMEM)


def smem():
    return pl.BlockSpec(memory_space=pltpu.SMEM)


def limit(mib):
    return pltpu.CompilerParams(vmem_limit_bytes=mib << 20)


def ring(size, step):
    return [(i, (i + step) % size) for i in range(size)]


def arrival(sizes, depth):
    z_size, x_size, yh_size = sizes
    rows = depth // (z_size * x_size * yh_size * 4)
    at = lax.broadcasted_iota(jnp.int32, (1, depth), 1)
    row, at = at % rows, at // rows
    yh, at = at % yh_size, at // yh_size
    z, at = at % z_size, at // z_size
    chip, x = at % 4, at // 4
    natural = (((z * x_size + x) * yh_size + yh) * 4 + chip) * rows + row
    index = lax.broadcasted_iota(jnp.int32, (depth, depth), 0)
    return jnp.where(index == natural, 1.0, 0.0).astype(BF16)


def message_kernel(sizes, order, features, qkv, out_t, message, own):
    position = lax.broadcasted_iota(jnp.int32, (order.shape[1],) * 2, 0)
    picks = jnp.where(position == order[...], 1.0, 0.0).T.astype(BF16)
    found = jnp.dot(picks, features[...], preferred_element_type=F32).astype(BF16)
    by_arrival = arrival(sizes, features.shape[1])
    own[...] = jnp.dot(found, by_arrival, preferred_element_type=F32).astype(BF16)
    rows, width = qkv.shape[0], qkv.shape[1] // 3
    lane = lax.broadcasted_iota(jnp.int32, (rows, BLK), 1)
    first = lane // HALF % 2 == 0
    parts = []
    for p in range(2):
        at = p * width // 2
        left = qkv[:, at : at + BLK].astype(F32)
        right = qkv[:, at + BLK : at + 2 * BLK].astype(F32)
        for c in range(2):
            if c == 0:
                query = jnp.where(first, left, pltpu.roll(right, HALF, 1))
            else:
                query = jnp.where(first, pltpu.roll(left, BLK - HALF, 1), right)
            from_kv = (1 + c) * width + p * width // 2
            parts += [qkv[:, from_kv : from_kv + width // 2], query.astype(BF16)]
    value = jnp.concatenate(parts + [out_t[...]], axis=-1)
    message[...] = jnp.broadcast_to(value[None], message.shape)


def spread_kernel(near, spread):
    used = spread.shape[2]
    for i in range(spread.shape[0]):
        at = i % 4 * used
        spread[i] = near[:, at : at + used]


def order_kernel(sizes, ringed, ringed_other, out, arrived):
    x_size, cores, rows, _ = ringed.shape
    here = {name: lax.axis_index(name) for name in ("x", "p", "c")}
    for ref, p in ((ringed, here["p"]), (ringed_other, 1 - here["p"])):
        for k in range(x_size):
            x = lax.rem(here["x"] + k, x_size)
            for i in range(cores):
                c = here["c"] if i == 0 else 1 - here["c"]
                at = pl.multiple_of(((x * 2 + p) * cores + c) * rows, rows)
                arrived[pl.ds(at, rows), :] = ref[k, i]
    by_arrival = arrival(sizes, arrived.shape[0])
    out[...] = jnp.dot(by_arrival, arrived[...], preferred_element_type=F32).astype(BF16)


def project_kernel(weight, *refs):
    mine, other, qkv_out = refs[:2], refs[2:4], refs[4]
    depth, used = weight.shape
    p, c = lax.axis_index("p"), lax.axis_index("c")
    heads = used // (HD + HALF)
    wide = heads * HD

    for blocks, at_c in ((mine, c), (other, 1 - c)):
        for side, pair in enumerate((blocks[0], blocks[1].at[0], blocks[1].at[1])):
            columns = used if side == 0 else wide
            to = 0 if side == 0 else HALF + side * HD
            result = jnp.dot(
                pair[...].reshape(2 * BLK, depth), weight[:, :columns], preferred_element_type=F32
            )
            flipped = result.astype(BF16).T
            for j in range(2):
                at_p = p if j == 0 else 1 - p
                lanes = pl.ds(pl.multiple_of((at_c * 2 + at_p) * BLK, BLK), BLK)
                part = flipped[:, j * BLK : (j + 1) * BLK]
                for head in range(heads):
                    qkv_out[head, to : to + HD, lanes] = part[head * HD : (head + 1) * HD]
                    if side == 0:
                        at = wide + (head % 2 * 2 + head // 2) * HALF
                        qkv_out[head, HD : HD + HALF, lanes] = part[at : at + HALF]


def attend_kernel(scale, units, lanes, counts, mine, other, out, scores):
    q_blocks = out.shape[0]
    slots = scores.shape[1]
    core = lax.axis_index("c")

    def attend(keys, values, low, high):
        def one_block(block, room):
            yh, p = block // 2, block % 2
            q_unit = yh * UNITS + 2
            q_lanes = pl.ds(pl.multiple_of((core * 2 + p) * BLK, BLK), BLK)
            query = jnp.concatenate([low[q_unit, :, q_lanes], high[q_unit, :, q_lanes]], axis=0).T
            count = counts[block]

            def tiles(ref, first):
                found = []
                for slot in range(first, first + UNROLL):
                    at = pl.ds(pl.multiple_of(lanes[block, slot], BLK), BLK)
                    found.append(ref[pl.ds(units[block, slot], 2), :, at].reshape(HD, BLK))
                return jnp.concatenate(found, axis=1)

            top = jnp.full((BLK, BLK), -1e30, F32)
            for first in range(0, slots, UNROLL):
                got = jnp.dot(query, tiles(keys, first), preferred_element_type=F32)
                got = got * (scale * LOG2_E)
                for i in range(UNROLL):
                    part = jnp.where(first + i < count, got[:, i * BLK : (i + 1) * BLK], -1e30)
                    scores[room, first + i] = part
                    top = jnp.maximum(top, part)
            top = jnp.max(top, axis=1, keepdims=True)

            total = jnp.zeros((BLK, BLK), F32)
            summed = jnp.zeros((BLK, HD), F32)
            for first in range(0, slots, UNROLL):
                soft = []
                for i in range(UNROLL):
                    part = jnp.exp2(scores[room, first + i] - top)
                    total = total + part
                    soft.append(part.astype(BF16))
                summed = summed + lax.dot_general(
                    jnp.concatenate(soft, axis=1), tiles(values, first), (((1,), (1,)), ((), ())),
                    preferred_element_type=F32,
                )
            total = jnp.sum(total, axis=1, keepdims=True)
            out[block] = (summed / total).T.astype(BF16)

        def several(step, carry):
            for room in range(TOGETHER):
                one_block(step * TOGETHER + room, room)
            return carry

        lax.fori_loop(0, q_blocks // TOGETHER, several, 0)

    @pl.when(core == 0)
    def _():
        attend(mine, other, mine, other)

    @pl.when(core == 1)
    def _():
        attend(other, mine, other, mine)


def mix_kernel(attended, weight, mixed):
    count = attended.shape[0] // 2
    heads = [attended[yh * 2 + p] for p in range(2) for yh in range(count)]
    mixed[...] = lax.dot_general(
        jnp.concatenate(heads, axis=0).T, weight[...], (((1,), (1,)), ((), ())),
        preferred_element_type=F32,
    ).astype(BF16)


def block_lists(neighbours, counts, c, slab, slabs, yh_size):
    ka_size = yh_size * 4
    listed = neighbours.reshape(yh_size * 2, 2, -1)
    listed = lax.dynamic_index_in_dim(listed, c, axis=1, keepdims=False)
    used = lax.dynamic_index_in_dim(counts.reshape(yh_size * 2, 2), c, axis=1, keepdims=False)
    side = (listed // ka_size - slab + 1 + slabs) % slabs
    along = listed % ka_size
    offset = jnp.where(side == 1, 0, jnp.where(side == 0, 3, 5))
    unit = along // 4 * UNITS + offset
    lane = (along % 2 * 2 + along // 2 % 2) * BLK
    is_used = jnp.arange(listed.shape[1])[None, :] < used[:, None]
    return (
        jnp.where(is_used, unit, 0).astype(jnp.int32),
        jnp.where(is_used, lane, 0).astype(jnp.int32),
        used,
    )


def body(features, order, neighbours, counts, qkv_weight, out_weight):
    dev_rows, depth = features.shape
    rows, width = qkv_weight.shape[0], qkv_weight.shape[1] // 3
    z_size, x_size, yh_size = (lax.axis_size(name) for name in ("z", "x", "yh"))
    slabs = z_size * x_size
    c = lax.axis_index("c")
    slab = lax.axis_index("z") * x_size + lax.axis_index("x")
    used_width = width * 3 // 4

    sizes = (z_size, x_size, yh_size)

    with jax.named_scope("weights_near"):
        message, own = pl.pallas_call(
            functools.partial(message_kernel, sizes),
            out_shape=(
                jax.ShapeDtypeStruct((z_size * yh_size, rows, 4 * width), BF16),
                jax.ShapeDtypeStruct(features.shape, BF16),
            ),
            in_specs=[vmem()] * 4,
            out_specs=(vmem(), vmem()),
            name="message",
        )(order.reshape(1, -1), features, qkv_weight, out_weight.T)

    with jax.named_scope("rows"):
        pair = jnp.stack([own, lax.ppermute(own, "p", ring(2, 1))])
        before = lax.ppermute(pair, ("z", "x"), ring(slabs, 1))
        after = lax.ppermute(pair, ("z", "x"), ring(slabs, -1))

    with jax.named_scope("weights_near"):
        near = lax.all_to_all(message, ("z", "yh"), 0, 0, tiled=True).reshape(-1, 4 * width)

    with jax.named_scope("lists"):
        lists = block_lists(neighbours, counts, c, slab, slabs, yh_size)
        near, lists, _ = lax.optimization_barrier((near, lists, pair))
        unit, lane, used = lists

    with jax.named_scope("weights_far"):
        spread = pl.pallas_call(
            spread_kernel,
            out_shape=jax.ShapeDtypeStruct((x_size * 4, near.shape[0], used_width), BF16),
            in_specs=[vmem()],
            out_specs=vmem(),
            compiler_params=limit(16),
            name="spread",
        )(near)
        weight = lax.all_to_all(spread, ("x", "p", "c"), 0, 0, tiled=True).reshape(depth, -1)
        _, halo = lax.optimization_barrier((spread, (before, after)))
        mine = [pair, jnp.stack(halo)]
        other = [lax.ppermute(piece, "c", ring(2, 1)) for piece in mine]

    with jax.named_scope("project"):
        qkv = pl.pallas_call(
            project_kernel,
            out_shape=jax.ShapeDtypeStruct((yh_size, UNITS * HALF, 4 * dev_rows), BF16),
            in_specs=[vmem()] * 5,
            out_specs=vmem(),
            compiler_params=limit(24),
            name="project",
        )(weight, *mine, *other)
        qkv, near = lax.optimization_barrier((qkv, near))

    with jax.named_scope("heads"):
        mine = lax.all_to_all(qkv, "yh", 0, 0, tiled=True)

    with jax.named_scope("out_weight"):
        near_out = near[:, 3 * width :]
        chip = jnp.stack([near_out, lax.ppermute(near_out, "c", ring(2, 1))])
        ringed = [chip] + [lax.ppermute(chip, "x", ring(x_size, -k)) for k in range(1, x_size)]
        ringed = jnp.stack(ringed)
        mine, _ = lax.optimization_barrier((mine, ringed))
        mine = mine.reshape(-1, HALF, 4 * dev_rows)
        ringed_other = lax.ppermute(ringed, "p", ring(2, 1))

    with jax.named_scope("attend"):
        other = lax.ppermute(mine, "c", ring(2, 1))
        slots = -(-neighbours.shape[1] // UNROLL) * UNROLL
        attended = pl.pallas_call(
            functools.partial(attend_kernel, HD ** -0.5),
            out_shape=jax.ShapeDtypeStruct((yh_size * 2, HD, dev_rows), BF16),
            in_specs=[smem()] * 3 + [vmem()] * 2,
            out_specs=vmem(),
            scratch_shapes=[pltpu.VMEM((TOGETHER, slots, BLK, BLK), F32)],
            compiler_params=limit(24),
            name="attend",
        )(unit, lane, used, mine, other)

    with jax.named_scope("return"):
        _, arrived = lax.optimization_barrier((attended, (ringed, ringed_other)))
        attended = lax.all_to_all(attended, ("yh", "p"), 0, 0, tiled=True)

        mix_weight = pl.pallas_call(
            functools.partial(order_kernel, sizes),
            out_shape=jax.ShapeDtypeStruct((depth, width), BF16),
            in_specs=[vmem()] * 2,
            out_specs=vmem(),
            scratch_shapes=[pltpu.VMEM((depth, width), BF16)],
            compiler_params=limit(24),
            name="order",
        )(*arrived)

    with jax.named_scope("mix"):
        return pl.pallas_call(
            mix_kernel,
            out_shape=jax.ShapeDtypeStruct((dev_rows, depth), BF16),
            in_specs=[vmem()] * 2,
            out_specs=vmem(),
            compiler_params=limit(16),
            name="mix",
        )(attended, mix_weight)


def solution(mesh):
    pb_size, ka_size = mesh.shape["pb"], mesh.shape["ka"]
    shape = (pb_size // CHIPS_X, CHIPS_X, ka_size // CORES // 2, 2, CORES)
    fine = Mesh(mesh.devices.reshape(shape), ALL)
    return jax.shard_map(
        body,
        mesh=fine,
        in_specs=(
            P(ALL, None),
            P(ALL),
            P(("z", "x"), None),
            P(("z", "x")),
            P(ALL, None),
            P(None, ALL),
        ),
        out_specs=P(ALL, None),
        check_vma=False,
    )
```

```python
import functools

import jax
import jax.numpy as jnp
from jax import lax
from jax.experimental import pallas as pl
from jax.experimental.pallas import tpu as pltpu
from jax.sharding import Mesh, PartitionSpec as P

HD = 64
HALF = HD // 2
BLK = 128
UNROLL = 4
TOGETHER = 8
CHIPS_X = 4
CORES = 2
LOG2_E = 1.4426950408889634
ALL = ("z", "x", "yh", "p", "c")
BF16 = jnp.bfloat16
F32 = jnp.float32

UNITS = 7


def vmem():
    return pl.BlockSpec(memory_space=pltpu.VMEM)


def smem():
    return pl.BlockSpec(memory_space=pltpu.SMEM)


def limit(mib):
    return pltpu.CompilerParams(vmem_limit_bytes=mib << 20)


def ring(size, step):
    return [(i, (i + step) % size) for i in range(size)]


def arrival(sizes, depth):
    z_size, x_size, yh_size = sizes
    rows = depth // (z_size * x_size * yh_size * 4)
    at = lax.broadcasted_iota(jnp.int32, (1, depth), 1)
    row, at = at % rows, at // rows
    p, at = at % 2, at // 2
    yh, at = at % yh_size, at // yh_size
    z, at = at % z_size, at // z_size
    c, x = at % 2, at // 2
    natural = (((z * x_size + x) * yh_size + yh) * 4 + p * 2 + c) * rows + row
    index = lax.broadcasted_iota(jnp.int32, (depth, depth), 0)
    return jnp.where(index == natural, 1.0, 0.0).astype(BF16)


def message_kernel(sizes, order, features, qkv, out_t, message, own):
    position = lax.broadcasted_iota(jnp.int32, (order.shape[1],) * 2, 0)
    picks = jnp.where(position == order[...], 1.0, 0.0).T.astype(BF16)
    found = jnp.dot(picks, features[...], preferred_element_type=F32).astype(BF16)
    by_arrival = arrival(sizes, features.shape[1])
    own[...] = jnp.dot(found, by_arrival, preferred_element_type=F32).astype(BF16)
    rows, width = qkv.shape[0], qkv.shape[1] // 3
    lane = lax.broadcasted_iota(jnp.int32, (rows, BLK), 1)
    first = lane // HALF % 2 == 0
    for p in range(2):
        parts = []
        at = p * width // 2
        left = qkv[:, at : at + BLK].astype(F32)
        right = qkv[:, at + BLK : at + 2 * BLK].astype(F32)
        for c in range(2):
            if c == 0:
                query = jnp.where(first, left, pltpu.roll(right, HALF, 1))
            else:
                query = jnp.where(first, pltpu.roll(left, BLK - HALF, 1), right)
            from_kv = (1 + c) * width + p * width // 2
            parts += [qkv[:, from_kv : from_kv + width // 2], query.astype(BF16)]
        value = jnp.concatenate(parts + [out_t[...]], axis=-1)
        message[:, p] = jnp.broadcast_to(value[None], (message.shape[0],) + value.shape)


def spread_kernel(near, spread):
    used = spread.shape[2]
    for i in range(spread.shape[0]):
        at = i % 2 * used
        spread[i] = near[:, at : at + used]


def order_kernel(sizes, *refs):
    pieces, out, arrived = refs[:-2], refs[-2], refs[-1]
    cores, rows, _ = pieces[0].shape
    for k, piece in enumerate(pieces):
        x = lax.rem(lax.axis_index("x") + k, len(pieces))
        for i in range(cores):
            c = lax.axis_index("c") if i == 0 else 1 - lax.axis_index("c")
            at = pl.multiple_of((x * cores + c) * rows, rows)
            arrived[pl.ds(at, rows), :] = piece[i]
    by_arrival = arrival(sizes, arrived.shape[0])
    out[...] = jnp.dot(by_arrival, arrived[...], preferred_element_type=F32).astype(BF16)


def project_kernel(weight, *refs):
    mine, other, qkv_out = refs[:3], refs[3:6], refs[6]
    depth, used = weight.shape
    p, c = lax.axis_index("p"), lax.axis_index("c")
    heads = used // (HD + HALF)
    wide = heads * HD

    for blocks, at_c in ((mine, c), (other, 1 - c)):
        for side, pair in enumerate(blocks):
            columns = used if side == 0 else wide
            to = 0 if side == 0 else HALF + side * HD
            result = jnp.dot(
                pair[...].reshape(2 * BLK, depth), weight[:, :columns], preferred_element_type=F32
            )
            flipped = result.astype(BF16).T
            for j in range(2):
                at_p = p if j == 0 else 1 - p
                lanes = pl.ds(pl.multiple_of((at_c * 2 + at_p) * BLK, BLK), BLK)
                part = flipped[:, j * BLK : (j + 1) * BLK]
                for head in range(heads):
                    qkv_out[head, to : to + HD, lanes] = part[head * HD : (head + 1) * HD]
                    if side == 0:
                        at = wide + (head % 2 * 2 + head // 2) * HALF
                        qkv_out[head, HD : HD + HALF, lanes] = part[at : at + HALF]


def attend_kernel(scale, units, lanes, counts, mine, other, out, scores):
    q_blocks = out.shape[0]
    slots = scores.shape[1]
    core = lax.axis_index("c")

    def attend(keys, values, low, high):
        def one_block(block, room):
            yh, p = block // 2, block % 2
            q_unit = yh * UNITS + 2
            q_lanes = pl.ds(pl.multiple_of((core * 2 + p) * BLK, BLK), BLK)
            query = jnp.concatenate([low[q_unit, :, q_lanes], high[q_unit, :, q_lanes]], axis=0).T
            count = counts[block]

            def tiles(ref, first):
                found = []
                for slot in range(first, first + UNROLL):
                    at = pl.ds(pl.multiple_of(lanes[block, slot], BLK), BLK)
                    found.append(ref[pl.ds(units[block, slot], 2), :, at].reshape(HD, BLK))
                return jnp.concatenate(found, axis=1)

            top = jnp.full((BLK, BLK), -1e30, F32)
            for first in range(0, slots, UNROLL):
                got = jnp.dot(query, tiles(keys, first), preferred_element_type=F32)
                got = got * (scale * LOG2_E)
                for i in range(UNROLL):
                    part = jnp.where(first + i < count, got[:, i * BLK : (i + 1) * BLK], -1e30)
                    scores[room, first + i] = part
                    top = jnp.maximum(top, part)
            top = jnp.max(top, axis=1, keepdims=True)

            total = jnp.zeros((BLK, BLK), F32)
            summed = jnp.zeros((BLK, HD), F32)
            for first in range(0, slots, UNROLL):
                soft = []
                for i in range(UNROLL):
                    part = jnp.exp2(scores[room, first + i] - top)
                    total = total + part
                    soft.append(part.astype(BF16))
                summed = summed + lax.dot_general(
                    jnp.concatenate(soft, axis=1), tiles(values, first), (((1,), (1,)), ((), ())),
                    preferred_element_type=F32,
                )
            total = jnp.sum(total, axis=1, keepdims=True)
            out[block] = (summed / total).T.astype(BF16)

        def several(step, carry):
            for room in range(TOGETHER):
                one_block(step * TOGETHER + room, room)
            return carry

        lax.fori_loop(0, q_blocks // TOGETHER, several, 0)

    @pl.when(core == 0)
    def _():
        attend(mine, other, mine, other)

    @pl.when(core == 1)
    def _():
        attend(other, mine, other, mine)


def mix_kernel(attended, weight, mixed):
    count = attended.shape[0] // 2
    heads = [attended[yh * 2 + p] for p in range(2) for yh in range(count)]
    mixed[...] = lax.dot_general(
        jnp.concatenate(heads, axis=0).T, weight[...], (((1,), (1,)), ((), ())),
        preferred_element_type=F32,
    ).astype(BF16)


def block_lists(neighbours, counts, c, slab, slabs, yh_size):
    ka_size = yh_size * 4
    listed = neighbours.reshape(yh_size * 2, 2, -1)
    listed = lax.dynamic_index_in_dim(listed, c, axis=1, keepdims=False)
    used = lax.dynamic_index_in_dim(counts.reshape(yh_size * 2, 2), c, axis=1, keepdims=False)
    side = (listed // ka_size - slab + 1 + slabs) % slabs
    along = listed % ka_size
    offset = jnp.where(side == 1, 0, jnp.where(side == 0, 3, 5))
    unit = along // 4 * UNITS + offset
    lane = (along % 2 * 2 + along // 2 % 2) * BLK
    is_used = jnp.arange(listed.shape[1])[None, :] < used[:, None]
    return (
        jnp.where(is_used, unit, 0).astype(jnp.int32),
        jnp.where(is_used, lane, 0).astype(jnp.int32),
        used,
    )


def body(features, order, neighbours, counts, qkv_weight, out_weight):
    dev_rows, depth = features.shape
    rows, width = qkv_weight.shape[0], qkv_weight.shape[1] // 3
    z_size, x_size, yh_size = (lax.axis_size(name) for name in ("z", "x", "yh"))
    slabs = z_size * x_size
    c = lax.axis_index("c")
    slab = lax.axis_index("z") * x_size + lax.axis_index("x")
    used_width = width * 3 // 4

    sizes = (z_size, x_size, yh_size)
    near_width = 2 * used_width + width

    with jax.named_scope("weights_near"):
        message, own = pl.pallas_call(
            functools.partial(message_kernel, sizes),
            out_shape=(
                jax.ShapeDtypeStruct((z_size * yh_size, 2, rows, near_width), BF16),
                jax.ShapeDtypeStruct(features.shape, BF16),
            ),
            in_specs=[vmem()] * 4,
            out_specs=(vmem(), vmem()),
            name="message",
        )(order.reshape(1, -1), features, qkv_weight, out_weight.T)

    with jax.named_scope("rows"):
        pair = jnp.stack([own, lax.ppermute(own, "p", ring(2, 1))])
        before = lax.ppermute(pair, ("z", "x"), ring(slabs, 1))
        after = lax.ppermute(pair, ("z", "x"), ring(slabs, -1))

    with jax.named_scope("weights_near"):
        message = message.reshape(-1, rows, near_width)
        near = lax.all_to_all(message, ("z", "yh", "p"), 0, 0, tiled=True)
        near = near.reshape(-1, near_width)

    with jax.named_scope("lists"):
        lists = block_lists(neighbours, counts, c, slab, slabs, yh_size)
        near, lists, _ = lax.optimization_barrier((near, lists, pair))
        unit, lane, used = lists

    with jax.named_scope("weights_far"):
        spread = pl.pallas_call(
            spread_kernel,
            out_shape=jax.ShapeDtypeStruct((x_size * 2, near.shape[0], used_width), BF16),
            in_specs=[vmem()],
            out_specs=vmem(),
            compiler_params=limit(16),
            name="spread",
        )(near)
        weight = lax.all_to_all(spread, ("x", "c"), 0, 0, tiled=True).reshape(depth, -1)
        _, mine = lax.optimization_barrier((spread, (pair, before, after)))
        other = [lax.ppermute(piece, "c", ring(2, 1)) for piece in mine]

    with jax.named_scope("project"):
        qkv = pl.pallas_call(
            project_kernel,
            out_shape=jax.ShapeDtypeStruct((yh_size, UNITS * HALF, 4 * dev_rows), BF16),
            in_specs=[vmem()] * 7,
            out_specs=vmem(),
            compiler_params=limit(24),
            name="project",
        )(weight, *mine, *other)
        qkv, near = lax.optimization_barrier((qkv, near))

    with jax.named_scope("heads"):
        mine = lax.all_to_all(qkv, "yh", 0, 0, tiled=True)

    with jax.named_scope("out_weight"):
        near_out = near[:, 2 * used_width :]
        chip = jnp.stack([near_out, lax.ppermute(near_out, "c", ring(2, 1))])
        pieces = [chip] + [lax.ppermute(chip, "x", ring(x_size, -k)) for k in range(1, x_size)]
        mine, pieces = lax.optimization_barrier((mine, pieces))
        mine = mine.reshape(-1, HALF, 4 * dev_rows)

    with jax.named_scope("attend"):
        other = lax.ppermute(mine, "c", ring(2, 1))
        slots = -(-neighbours.shape[1] // UNROLL) * UNROLL
        attended = pl.pallas_call(
            functools.partial(attend_kernel, HD ** -0.5),
            out_shape=jax.ShapeDtypeStruct((yh_size * 2, HD, dev_rows), BF16),
            in_specs=[smem()] * 3 + [vmem()] * 2,
            out_specs=vmem(),
            scratch_shapes=[pltpu.VMEM((TOGETHER, slots, BLK, BLK), F32)],
            compiler_params=limit(24),
            name="attend",
        )(unit, lane, used, mine, other)

    with jax.named_scope("return"):
        _, pieces = lax.optimization_barrier((attended, pieces))
        attended = lax.all_to_all(attended, ("yh", "p"), 0, 0, tiled=True)

        mix_weight = pl.pallas_call(
            functools.partial(order_kernel, sizes),
            out_shape=jax.ShapeDtypeStruct((depth, width), BF16),
            in_specs=[vmem()] * x_size,
            out_specs=vmem(),
            scratch_shapes=[pltpu.VMEM((depth, width), BF16)],
            compiler_params=limit(24),
            name="order",
        )(*pieces)

    with jax.named_scope("mix"):
        return pl.pallas_call(
            mix_kernel,
            out_shape=jax.ShapeDtypeStruct((dev_rows, depth), BF16),
            in_specs=[vmem()] * 2,
            out_specs=vmem(),
            compiler_params=limit(16),
            name="mix",
        )(attended, mix_weight)


def solution(mesh):
    pb_size, ka_size = mesh.shape["pb"], mesh.shape["ka"]
    shape = (pb_size // CHIPS_X, CHIPS_X, ka_size // CORES // 2, 2, CORES)
    fine = Mesh(mesh.devices.reshape(shape), ALL)
    return jax.shard_map(
        body,
        mesh=fine,
        in_specs=(
            P(ALL, None),
            P(ALL),
            P(("z", "x"), None),
            P(("z", "x")),
            P(ALL, None),
            P(None, ALL),
        ),
        out_specs=P(ALL, None),
        check_vma=False,
    )
```

```python
import functools

import jax
import jax.numpy as jnp
from jax import lax
from jax.experimental import pallas as pl
from jax.experimental.pallas import tpu as pltpu
from jax.sharding import Mesh, PartitionSpec as P

HD = 64
HALF = HD // 2
BLK = 128
UNROLL = 4
TOGETHER = 8
CHIPS_X = 4
CORES = 2
LOG2_E = 1.4426950408889634
ALL = ("z", "x", "yh", "p", "c")
BF16 = jnp.bfloat16
F32 = jnp.float32

UNITS = 7


def vmem():
    return pl.BlockSpec(memory_space=pltpu.VMEM)


def smem():
    return pl.BlockSpec(memory_space=pltpu.SMEM)


def limit(mib):
    return pltpu.CompilerParams(vmem_limit_bytes=mib << 20)


def ring(size, step):
    return [(i, (i + step) % size) for i in range(size)]


def arrival(sizes, depth):
    z_size, x_size, yh_size = sizes
    rows = depth // (z_size * x_size * yh_size * 4)
    at = lax.broadcasted_iota(jnp.int32, (1, depth), 1)
    row, at = at % rows, at // rows
    p, at = at % 2, at // 2
    yh, at = at % yh_size, at // yh_size
    z, at = at % z_size, at // z_size
    c, x = at % 2, at // 2
    natural = (((z * x_size + x) * yh_size + yh) * 4 + p * 2 + c) * rows + row
    index = lax.broadcasted_iota(jnp.int32, (depth, depth), 0)
    return jnp.where(index == natural, 1.0, 0.0).astype(BF16)


def message_kernel(sizes, order, features, qkv, out_t, message, own):
    position = lax.broadcasted_iota(jnp.int32, (order.shape[1],) * 2, 0)
    picks = jnp.where(position == order[...], 1.0, 0.0).T.astype(BF16)
    found = jnp.dot(picks, features[...], preferred_element_type=F32).astype(BF16)
    by_arrival = arrival(sizes, features.shape[1])
    own[...] = jnp.dot(found, by_arrival, preferred_element_type=F32).astype(BF16)
    rows, width = qkv.shape[0], qkv.shape[1] // 3
    lane = lax.broadcasted_iota(jnp.int32, (rows, BLK), 1)
    first = lane // HALF % 2 == 0
    for p in range(2):
        parts = []
        at = p * width // 2
        left = qkv[:, at : at + BLK].astype(F32)
        right = qkv[:, at + BLK : at + 2 * BLK].astype(F32)
        for c in range(2):
            if c == 0:
                query = jnp.where(first, left, pltpu.roll(right, HALF, 1))
            else:
                query = jnp.where(first, pltpu.roll(left, BLK - HALF, 1), right)
            from_kv = (1 + c) * width + p * width // 2
            parts += [qkv[:, from_kv : from_kv + width // 2], query.astype(BF16)]
        value = jnp.concatenate(parts + [out_t[...]], axis=-1)
        message[:, p] = jnp.broadcast_to(value[None], (message.shape[0],) + value.shape)


def spread_kernel(near, spread):
    used = spread.shape[2]
    for i in range(spread.shape[0]):
        at = i % 2 * used
        spread[i] = near[:, at : at + used]


def order_kernel(sizes, mine, other, out, arrived):
    x_size, rows, _ = mine.shape
    for ref, c in ((mine, lax.axis_index("c")), (other, 1 - lax.axis_index("c"))):
        for k in range(x_size):
            x = lax.rem(lax.axis_index("x") + k, x_size)
            at = pl.multiple_of((x * 2 + c) * rows, rows)
            arrived[pl.ds(at, rows), :] = ref[k]
    by_arrival = arrival(sizes, arrived.shape[0])
    out[...] = jnp.dot(by_arrival, arrived[...], preferred_element_type=F32).astype(BF16)


def project_kernel(weight, *refs):
    mine, other, qkv_out = refs[:3], refs[3:6], refs[6]
    depth, used = weight.shape
    p, c = lax.axis_index("p"), lax.axis_index("c")
    heads = used // (HD + HALF)
    wide = heads * HD

    for blocks, at_c in ((mine, c), (other, 1 - c)):
        for side, pair in enumerate(blocks):
            columns = used if side == 0 else wide
            to = 0 if side == 0 else HALF + side * HD
            result = jnp.dot(
                pair[...].reshape(2 * BLK, depth), weight[:, :columns], preferred_element_type=F32
            )
            flipped = result.astype(BF16).T
            for j in range(2):
                at_p = p if j == 0 else 1 - p
                lanes = pl.ds(pl.multiple_of((at_c * 2 + at_p) * BLK, BLK), BLK)
                part = flipped[:, j * BLK : (j + 1) * BLK]
                for head in range(heads):
                    qkv_out[head, to : to + HD, lanes] = part[head * HD : (head + 1) * HD]
                    if side == 0:
                        at = wide + (head % 2 * 2 + head // 2) * HALF
                        qkv_out[head, HD : HD + HALF, lanes] = part[at : at + HALF]


def attend_kernel(scale, units, lanes, counts, mine, other, out, scores):
    q_blocks = out.shape[0]
    slots = scores.shape[1]
    core = lax.axis_index("c")

    def attend(keys, values, low, high):
        def one_block(block, room):
            yh, p = block // 2, block % 2
            q_unit = yh * UNITS + 2
            q_lanes = pl.ds(pl.multiple_of((core * 2 + p) * BLK, BLK), BLK)
            query = jnp.concatenate([low[q_unit, :, q_lanes], high[q_unit, :, q_lanes]], axis=0).T
            count = counts[block]

            def tiles(ref, first):
                found = []
                for slot in range(first, first + UNROLL):
                    at = pl.ds(pl.multiple_of(lanes[block, slot], BLK), BLK)
                    found.append(ref[pl.ds(units[block, slot], 2), :, at].reshape(HD, BLK))
                return jnp.concatenate(found, axis=1)

            top = jnp.full((BLK, BLK), -1e30, F32)
            for first in range(0, slots, UNROLL):
                got = jnp.dot(query, tiles(keys, first), preferred_element_type=F32)
                got = got * (scale * LOG2_E)
                for i in range(UNROLL):
                    part = jnp.where(first + i < count, got[:, i * BLK : (i + 1) * BLK], -1e30)
                    scores[room, first + i] = part
                    top = jnp.maximum(top, part)
            top = jnp.max(top, axis=1, keepdims=True)

            total = jnp.zeros((BLK, BLK), F32)
            summed = jnp.zeros((BLK, HD), F32)
            for first in range(0, slots, UNROLL):
                soft = []
                for i in range(UNROLL):
                    part = jnp.exp2(scores[room, first + i] - top)
                    total = total + part
                    soft.append(part.astype(BF16))
                summed = summed + lax.dot_general(
                    jnp.concatenate(soft, axis=1), tiles(values, first), (((1,), (1,)), ((), ())),
                    preferred_element_type=F32,
                )
            total = jnp.sum(total, axis=1, keepdims=True)
            out[block] = (summed / total).T.astype(BF16)

        def several(step, carry):
            for room in range(TOGETHER):
                one_block(step * TOGETHER + room, room)
            return carry

        lax.fori_loop(0, q_blocks // TOGETHER, several, 0)

    @pl.when(core == 0)
    def _():
        attend(mine, other, mine, other)

    @pl.when(core == 1)
    def _():
        attend(other, mine, other, mine)


def mix_kernel(attended, weight, mixed):
    count = attended.shape[0] // 2
    heads = [attended[yh * 2 + p] for p in range(2) for yh in range(count)]
    mixed[...] = lax.dot_general(
        jnp.concatenate(heads, axis=0).T, weight[...], (((1,), (1,)), ((), ())),
        preferred_element_type=F32,
    ).astype(BF16)


def block_lists(neighbours, counts, c, slab, slabs, yh_size):
    ka_size = yh_size * 4
    listed = neighbours.reshape(yh_size * 2, 2, -1)
    listed = lax.dynamic_index_in_dim(listed, c, axis=1, keepdims=False)
    used = lax.dynamic_index_in_dim(counts.reshape(yh_size * 2, 2), c, axis=1, keepdims=False)
    side = (listed // ka_size - slab + 1 + slabs) % slabs
    along = listed % ka_size
    offset = jnp.where(side == 1, 0, jnp.where(side == 0, 3, 5))
    unit = along // 4 * UNITS + offset
    lane = (along % 2 * 2 + along // 2 % 2) * BLK
    is_used = jnp.arange(listed.shape[1])[None, :] < used[:, None]
    return (
        jnp.where(is_used, unit, 0).astype(jnp.int32),
        jnp.where(is_used, lane, 0).astype(jnp.int32),
        used,
    )


def body(features, order, neighbours, counts, qkv_weight, out_weight):
    dev_rows, depth = features.shape
    rows, width = qkv_weight.shape[0], qkv_weight.shape[1] // 3
    z_size, x_size, yh_size = (lax.axis_size(name) for name in ("z", "x", "yh"))
    slabs = z_size * x_size
    c = lax.axis_index("c")
    slab = lax.axis_index("z") * x_size + lax.axis_index("x")
    used_width = width * 3 // 4

    sizes = (z_size, x_size, yh_size)
    near_width = 2 * used_width + width

    with jax.named_scope("weights_near"):
        message, own = pl.pallas_call(
            functools.partial(message_kernel, sizes),
            out_shape=(
                jax.ShapeDtypeStruct((z_size * yh_size, 2, rows, near_width), BF16),
                jax.ShapeDtypeStruct(features.shape, BF16),
            ),
            in_specs=[vmem()] * 4,
            out_specs=(vmem(), vmem()),
            name="message",
        )(order.reshape(1, -1), features, qkv_weight, out_weight.T)

    with jax.named_scope("rows"):
        pair = jnp.stack([own, lax.ppermute(own, "p", ring(2, 1))])
        before = lax.ppermute(pair, ("z", "x"), ring(slabs, 1))
        after = lax.ppermute(pair, ("z", "x"), ring(slabs, -1))

    with jax.named_scope("weights_near"):
        message = message.reshape(-1, rows, near_width)
        near = lax.all_to_all(message, ("z", "yh", "p"), 0, 0, tiled=True)
        near = near.reshape(-1, near_width)

    with jax.named_scope("lists"):
        lists = block_lists(neighbours, counts, c, slab, slabs, yh_size)
        near, lists, _ = lax.optimization_barrier((near, lists, pair))
        unit, lane, used = lists

    with jax.named_scope("weights_far"):
        spread = pl.pallas_call(
            spread_kernel,
            out_shape=jax.ShapeDtypeStruct((x_size * 2, near.shape[0], used_width), BF16),
            in_specs=[vmem()],
            out_specs=vmem(),
            compiler_params=limit(16),
            name="spread",
        )(near)
        weight = lax.all_to_all(spread, ("x", "c"), 0, 0, tiled=True).reshape(depth, -1)
        _, mine = lax.optimization_barrier((spread, (pair, before, after)))
        other = [lax.ppermute(piece, "c", ring(2, 1)) for piece in mine]

    with jax.named_scope("project"):
        qkv = pl.pallas_call(
            project_kernel,
            out_shape=jax.ShapeDtypeStruct((yh_size, UNITS * HALF, 4 * dev_rows), BF16),
            in_specs=[vmem()] * 7,
            out_specs=vmem(),
            compiler_params=limit(24),
            name="project",
        )(weight, *mine, *other)
        qkv, near = lax.optimization_barrier((qkv, near))

    with jax.named_scope("heads"):
        mine = lax.all_to_all(qkv, "yh", 0, 0, tiled=True)

    with jax.named_scope("out_weight"):
        near_out = near[:, 2 * used_width :]
        ringed = [near_out] + [
            lax.ppermute(near_out, "x", ring(x_size, -k)) for k in range(1, x_size)
        ]
        ringed = jnp.stack(ringed)
        mine, _ = lax.optimization_barrier((mine, ringed))
        mine = mine.reshape(-1, HALF, 4 * dev_rows)
        ringed_other = lax.ppermute(ringed, "c", ring(2, 1))

    with jax.named_scope("attend"):
        other = lax.ppermute(mine, "c", ring(2, 1))
        slots = -(-neighbours.shape[1] // UNROLL) * UNROLL
        attended = pl.pallas_call(
            functools.partial(attend_kernel, HD ** -0.5),
            out_shape=jax.ShapeDtypeStruct((yh_size * 2, HD, dev_rows), BF16),
            in_specs=[smem()] * 3 + [vmem()] * 2,
            out_specs=vmem(),
            scratch_shapes=[pltpu.VMEM((TOGETHER, slots, BLK, BLK), F32)],
            compiler_params=limit(24),
            name="attend",
        )(unit, lane, used, mine, other)

    with jax.named_scope("return"):
        _, pieces = lax.optimization_barrier((attended, (ringed, ringed_other)))
        attended = lax.all_to_all(attended, ("yh", "p"), 0, 0, tiled=True)

        mix_weight = pl.pallas_call(
            functools.partial(order_kernel, sizes),
            out_shape=jax.ShapeDtypeStruct((depth, width), BF16),
            in_specs=[vmem()] * 2,
            out_specs=vmem(),
            scratch_shapes=[pltpu.VMEM((depth, width), BF16)],
            compiler_params=limit(24),
            name="order",
        )(*pieces)

    with jax.named_scope("mix"):
        return pl.pallas_call(
            mix_kernel,
            out_shape=jax.ShapeDtypeStruct((dev_rows, depth), BF16),
            in_specs=[vmem()] * 2,
            out_specs=vmem(),
            compiler_params=limit(16),
            name="mix",
        )(attended, mix_weight)


def solution(mesh):
    pb_size, ka_size = mesh.shape["pb"], mesh.shape["ka"]
    shape = (pb_size // CHIPS_X, CHIPS_X, ka_size // CORES // 2, 2, CORES)
    fine = Mesh(mesh.devices.reshape(shape), ALL)
    return jax.shard_map(
        body,
        mesh=fine,
        in_specs=(
            P(ALL, None),
            P(ALL),
            P(("z", "x"), None),
            P(("z", "x")),
            P(ALL, None),
            P(None, ALL),
        ),
        out_specs=P(ALL, None),
        check_vma=False,
    )
```

```python
import functools

import jax
import jax.numpy as jnp
from jax import lax
from jax.experimental import pallas as pl
from jax.experimental.pallas import tpu as pltpu
from jax.sharding import Mesh, PartitionSpec as P

HD = 64
HALF = HD // 2
BLK = 128
UNROLL = 4
TOGETHER = 8
CHIPS_X = 4
CORES = 2
LOG2_E = 1.4426950408889634
ALL = ("z", "x", "yh", "p", "c")
BF16 = jnp.bfloat16
F32 = jnp.float32

UNITS = 7


def vmem():
    return pl.BlockSpec(memory_space=pltpu.VMEM)


def smem():
    return pl.BlockSpec(memory_space=pltpu.SMEM)


def limit(mib):
    return pltpu.CompilerParams(vmem_limit_bytes=mib << 20)


def ring(size, step):
    return [(i, (i + step) % size) for i in range(size)]


def arrival(sizes, depth):
    z_size, x_size, yh_size = sizes
    rows = depth // (z_size * x_size * yh_size * 4)
    at = lax.broadcasted_iota(jnp.int32, (1, depth), 1)
    row, at = at % rows, at // rows
    p, at = at % 2, at // 2
    yh, at = at % yh_size, at // yh_size
    z, at = at % z_size, at // z_size
    c, x = at % 2, at // 2
    natural = (((z * x_size + x) * yh_size + yh) * 4 + p * 2 + c) * rows + row
    index = lax.broadcasted_iota(jnp.int32, (depth, depth), 0)
    return jnp.where(index == natural, 1.0, 0.0).astype(BF16)


def message_kernel(sizes, order, features, qkv, out_t, message, own):
    position = lax.broadcasted_iota(jnp.int32, (order.shape[1],) * 2, 0)
    picks = jnp.where(position == order[...], 1.0, 0.0).T.astype(BF16)
    found = jnp.dot(picks, features[...], preferred_element_type=F32).astype(BF16)
    by_arrival = arrival(sizes, features.shape[1])
    own[...] = jnp.dot(found, by_arrival, preferred_element_type=F32).astype(BF16)
    rows, width = qkv.shape[0], qkv.shape[1] // 3
    lane = lax.broadcasted_iota(jnp.int32, (rows, BLK), 1)
    first = lane // HALF % 2 == 0
    for p in range(2):
        parts = []
        at = p * width // 2
        left = qkv[:, at : at + BLK].astype(F32)
        right = qkv[:, at + BLK : at + 2 * BLK].astype(F32)
        for c in range(2):
            if c == 0:
                query = jnp.where(first, left, pltpu.roll(right, HALF, 1))
            else:
                query = jnp.where(first, pltpu.roll(left, BLK - HALF, 1), right)
            from_kv = (1 + c) * width + p * width // 2
            parts += [qkv[:, from_kv : from_kv + width // 2], query.astype(BF16)]
        value = jnp.concatenate(parts + [out_t[...]], axis=-1)
        message[:, p] = jnp.broadcast_to(value[None], (message.shape[0],) + value.shape)


def spread_kernel(near, spread):
    used = spread.shape[2]
    for i in range(spread.shape[0]):
        at = i % 2 * used
        spread[i] = near[:, at : at + used]


def order_kernel(sizes, mine, other, out, arrived):
    x_size, rows, _ = mine.shape
    for ref, c in ((mine, lax.axis_index("c")), (other, 1 - lax.axis_index("c"))):
        for k in range(x_size):
            x = lax.rem(lax.axis_index("x") + k, x_size)
            at = pl.multiple_of((x * 2 + c) * rows, rows)
            arrived[pl.ds(at, rows), :] = ref[k]
    by_arrival = arrival(sizes, arrived.shape[0])
    out[...] = jnp.dot(by_arrival, arrived[...], preferred_element_type=F32).astype(BF16)


def project_kernel(is_last, weight, *refs):
    blocks, qkv_out = refs[:3], refs[-1]
    depth, used = weight.shape
    p, c = lax.axis_index("p"), lax.axis_index("c")
    heads = used // (HD + HALF)
    wide = heads * HD
    if is_last:
        earlier = refs[3]
        qkv_out[:, :, pl.ds(pl.multiple_of(c * 2 * BLK, 2 * BLK), 2 * BLK)] = earlier[...]

    for side, pair in enumerate(blocks):
        columns = used if side == 0 else wide
        to = 0 if side == 0 else HALF + side * HD
        result = jnp.dot(
            pair[...].reshape(2 * BLK, depth), weight[:, :columns], preferred_element_type=F32
        )
        flipped = result.astype(BF16).T
        for j in range(2):
            at = p if j == 0 else 1 - p
            if is_last:
                at = at + (1 - c) * 2
            lanes = pl.ds(pl.multiple_of(at * BLK, BLK), BLK)
            part = flipped[:, j * BLK : (j + 1) * BLK]
            for head in range(heads):
                qkv_out[head, to : to + HD, lanes] = part[head * HD : (head + 1) * HD]
                if side == 0:
                    at = wide + (head % 2 * 2 + head // 2) * HALF
                    qkv_out[head, HD : HD + HALF, lanes] = part[at : at + HALF]


def attend_kernel(scale, units, lanes, counts, mine, other, out, scores):
    q_blocks = out.shape[0]
    slots = scores.shape[1]
    core = lax.axis_index("c")

    def attend(keys, values, low, high):
        def one_block(block, room):
            yh, p = block // 2, block % 2
            q_unit = yh * UNITS + 2
            q_lanes = pl.ds(pl.multiple_of((core * 2 + p) * BLK, BLK), BLK)
            query = jnp.concatenate([low[q_unit, :, q_lanes], high[q_unit, :, q_lanes]], axis=0).T
            count = counts[block]

            def tiles(ref, first):
                found = []
                for slot in range(first, first + UNROLL):
                    at = pl.ds(pl.multiple_of(lanes[block, slot], BLK), BLK)
                    found.append(ref[pl.ds(units[block, slot], 2), :, at].reshape(HD, BLK))
                return jnp.concatenate(found, axis=1)

            top = jnp.full((BLK, BLK), -1e30, F32)
            for first in range(0, slots, UNROLL):
                got = jnp.dot(query, tiles(keys, first), preferred_element_type=F32)
                got = got * (scale * LOG2_E)
                for i in range(UNROLL):
                    part = jnp.where(first + i < count, got[:, i * BLK : (i + 1) * BLK], -1e30)
                    scores[room, first + i] = part
                    top = jnp.maximum(top, part)
            top = jnp.max(top, axis=1, keepdims=True)

            total = jnp.zeros((BLK, BLK), F32)
            summed = jnp.zeros((BLK, HD), F32)
            for first in range(0, slots, UNROLL):
                soft = []
                for i in range(UNROLL):
                    part = jnp.exp2(scores[room, first + i] - top)
                    total = total + part
                    soft.append(part.astype(BF16))
                summed = summed + lax.dot_general(
                    jnp.concatenate(soft, axis=1), tiles(values, first), (((1,), (1,)), ((), ())),
                    preferred_element_type=F32,
                )
            total = jnp.sum(total, axis=1, keepdims=True)
            out[block] = (summed / total).T.astype(BF16)

        def several(step, carry):
            for room in range(TOGETHER):
                one_block(step * TOGETHER + room, room)
            return carry

        lax.fori_loop(0, q_blocks // TOGETHER, several, 0)

    @pl.when(core == 0)
    def _():
        attend(mine, other, mine, other)

    @pl.when(core == 1)
    def _():
        attend(other, mine, other, mine)


def mix_kernel(attended, weight, mixed):
    count = attended.shape[0] // 2
    heads = [attended[yh * 2 + p] for p in range(2) for yh in range(count)]
    mixed[...] = lax.dot_general(
        jnp.concatenate(heads, axis=0).T, weight[...], (((1,), (1,)), ((), ())),
        preferred_element_type=F32,
    ).astype(BF16)


def block_lists(neighbours, counts, c, slab, slabs, yh_size):
    ka_size = yh_size * 4
    listed = neighbours.reshape(yh_size * 2, 2, -1)
    listed = lax.dynamic_index_in_dim(listed, c, axis=1, keepdims=False)
    used = lax.dynamic_index_in_dim(counts.reshape(yh_size * 2, 2), c, axis=1, keepdims=False)
    side = (listed // ka_size - slab + 1 + slabs) % slabs
    along = listed % ka_size
    offset = jnp.where(side == 1, 0, jnp.where(side == 0, 3, 5))
    unit = along // 4 * UNITS + offset
    lane = (along % 2 * 2 + along // 2 % 2) * BLK
    is_used = jnp.arange(listed.shape[1])[None, :] < used[:, None]
    return (
        jnp.where(is_used, unit, 0).astype(jnp.int32),
        jnp.where(is_used, lane, 0).astype(jnp.int32),
        used,
    )


def body(features, order, neighbours, counts, qkv_weight, out_weight):
    dev_rows, depth = features.shape
    rows, width = qkv_weight.shape[0], qkv_weight.shape[1] // 3
    z_size, x_size, yh_size = (lax.axis_size(name) for name in ("z", "x", "yh"))
    slabs = z_size * x_size
    c = lax.axis_index("c")
    slab = lax.axis_index("z") * x_size + lax.axis_index("x")
    used_width = width * 3 // 4

    sizes = (z_size, x_size, yh_size)
    near_width = 2 * used_width + width

    with jax.named_scope("weights_near"):
        message, own = pl.pallas_call(
            functools.partial(message_kernel, sizes),
            out_shape=(
                jax.ShapeDtypeStruct((z_size * yh_size, 2, rows, near_width), BF16),
                jax.ShapeDtypeStruct(features.shape, BF16),
            ),
            in_specs=[vmem()] * 4,
            out_specs=(vmem(), vmem()),
            name="message",
        )(order.reshape(1, -1), features, qkv_weight, out_weight.T)

    with jax.named_scope("rows"):
        pair = jnp.stack([own, lax.ppermute(own, "p", ring(2, 1))])
        before = lax.ppermute(pair, ("z", "x"), ring(slabs, 1))
        after = lax.ppermute(pair, ("z", "x"), ring(slabs, -1))

    with jax.named_scope("weights_near"):
        message = message.reshape(-1, rows, near_width)
        near = lax.all_to_all(message, ("z", "yh", "p"), 0, 0, tiled=True)
        near = near.reshape(-1, near_width)

    with jax.named_scope("lists"):
        lists = block_lists(neighbours, counts, c, slab, slabs, yh_size)
        near, lists, _ = lax.optimization_barrier((near, lists, pair))
        unit, lane, used = lists

    with jax.named_scope("weights_far"):
        spread = pl.pallas_call(
            spread_kernel,
            out_shape=jax.ShapeDtypeStruct((x_size * 2, near.shape[0], used_width), BF16),
            in_specs=[vmem()],
            out_specs=vmem(),
            compiler_params=limit(16),
            name="spread",
        )(near)
        weight = lax.all_to_all(spread, ("x", "c"), 0, 0, tiled=True).reshape(depth, -1)
        _, mine = lax.optimization_barrier((spread, (pair, before, after)))
        other = [lax.ppermute(piece, "c", ring(2, 1)) for piece in mine]

    with jax.named_scope("project"):

        def project(lanes, *operands):
            return pl.pallas_call(
                functools.partial(project_kernel, len(operands) == 5),
                out_shape=jax.ShapeDtypeStruct((yh_size, UNITS * HALF, lanes), BF16),
                in_specs=[vmem()] * len(operands),
                out_specs=vmem(),
                compiler_params=limit(24),
                name="project",
            )(*operands)

        qkv = project(2 * dev_rows, weight, *mine)
        qkv = project(4 * dev_rows, weight, *other, qkv)
        qkv, near = lax.optimization_barrier((qkv, near))

    with jax.named_scope("heads"):
        mine = lax.all_to_all(qkv, "yh", 0, 0, tiled=True)

    with jax.named_scope("out_weight"):
        near_out = near[:, 2 * used_width :]
        ringed = [near_out] + [
            lax.ppermute(near_out, "x", ring(x_size, -k)) for k in range(1, x_size)
        ]
        ringed = jnp.stack(ringed)
        mine, _ = lax.optimization_barrier((mine, ringed))
        mine = mine.reshape(-1, HALF, 4 * dev_rows)
        ringed_other = lax.ppermute(ringed, "c", ring(2, 1))

    with jax.named_scope("attend"):
        other = lax.ppermute(mine, "c", ring(2, 1))
        slots = -(-neighbours.shape[1] // UNROLL) * UNROLL
        attended = pl.pallas_call(
            functools.partial(attend_kernel, HD ** -0.5),
            out_shape=jax.ShapeDtypeStruct((yh_size * 2, HD, dev_rows), BF16),
            in_specs=[smem()] * 3 + [vmem()] * 2,
            out_specs=vmem(),
            scratch_shapes=[pltpu.VMEM((TOGETHER, slots, BLK, BLK), F32)],
            compiler_params=limit(24),
            name="attend",
        )(unit, lane, used, mine, other)

    with jax.named_scope("return"):
        _, pieces = lax.optimization_barrier((attended, (ringed, ringed_other)))
        attended = lax.all_to_all(attended, ("yh", "p"), 0, 0, tiled=True)

        mix_weight = pl.pallas_call(
            functools.partial(order_kernel, sizes),
            out_shape=jax.ShapeDtypeStruct((depth, width), BF16),
            in_specs=[vmem()] * 2,
            out_specs=vmem(),
            scratch_shapes=[pltpu.VMEM((depth, width), BF16)],
            compiler_params=limit(24),
            name="order",
        )(*pieces)

    with jax.named_scope("mix"):
        return pl.pallas_call(
            mix_kernel,
            out_shape=jax.ShapeDtypeStruct((dev_rows, depth), BF16),
            in_specs=[vmem()] * 2,
            out_specs=vmem(),
            compiler_params=limit(16),
            name="mix",
        )(attended, mix_weight)


def solution(mesh):
    pb_size, ka_size = mesh.shape["pb"], mesh.shape["ka"]
    shape = (pb_size // CHIPS_X, CHIPS_X, ka_size // CORES // 2, 2, CORES)
    fine = Mesh(mesh.devices.reshape(shape), ALL)
    return jax.shard_map(
        body,
        mesh=fine,
        in_specs=(
            P(ALL, None),
            P(ALL),
            P(("z", "x"), None),
            P(("z", "x")),
            P(ALL, None),
            P(None, ALL),
        ),
        out_specs=P(ALL, None),
        check_vma=False,
    )
```

```python
import functools

import jax
import jax.numpy as jnp
from jax import lax
from jax.experimental import pallas as pl
from jax.experimental.pallas import tpu as pltpu
from jax.sharding import Mesh, PartitionSpec as P

HD = 64
HALF = HD // 2
BLK = 128
UNROLL = 4
TOGETHER = 8
CHIPS_X = 4
CORES = 2
LOG2_E = 1.4426950408889634
ALL = ("z", "x", "yh", "p", "c")
BF16 = jnp.bfloat16
F32 = jnp.float32

UNITS = 7


def vmem():
    return pl.BlockSpec(memory_space=pltpu.VMEM)


def smem():
    return pl.BlockSpec(memory_space=pltpu.SMEM)


def limit(mib):
    return pltpu.CompilerParams(vmem_limit_bytes=mib << 20)


def ring(size, step):
    return [(i, (i + step) % size) for i in range(size)]


def arrival(sizes, depth):
    z_size, x_size, yh_size = sizes
    rows = depth // (z_size * x_size * yh_size * 4)
    at = lax.broadcasted_iota(jnp.int32, (1, depth), 1)
    row, at = at % rows, at // rows
    p, at = at % 2, at // 2
    yh, at = at % yh_size, at // yh_size
    z, at = at % z_size, at // z_size
    c, x = at % 2, at // 2
    natural = (((z * x_size + x) * yh_size + yh) * 4 + p * 2 + c) * rows + row
    index = lax.broadcasted_iota(jnp.int32, (depth, depth), 0)
    return jnp.where(index == natural, 1.0, 0.0).astype(BF16)


def message_kernel(sizes, order, features, qkv, out_t, message, own):
    position = lax.broadcasted_iota(jnp.int32, (order.shape[1],) * 2, 0)
    picks = jnp.where(position == order[...], 1.0, 0.0).T.astype(BF16)
    found = jnp.dot(picks, features[...], preferred_element_type=F32).astype(BF16)
    by_arrival = arrival(sizes, features.shape[1])
    own[...] = jnp.dot(found, by_arrival, preferred_element_type=F32).astype(BF16)
    rows, width = qkv.shape[0], qkv.shape[1] // 3
    lane = lax.broadcasted_iota(jnp.int32, (rows, BLK), 1)
    first = lane // HALF % 2 == 0
    for p in range(2):
        parts = []
        at = p * width // 2
        left = qkv[:, at : at + BLK].astype(F32)
        right = qkv[:, at + BLK : at + 2 * BLK].astype(F32)
        for c in range(2):
            if c == 0:
                query = jnp.where(first, left, pltpu.roll(right, HALF, 1))
            else:
                query = jnp.where(first, pltpu.roll(left, BLK - HALF, 1), right)
            from_kv = (1 + c) * width + p * width // 2
            parts += [qkv[:, from_kv : from_kv + width // 2], query.astype(BF16)]
        value = jnp.concatenate(parts + [out_t[...]], axis=-1)
        message[:, p] = jnp.broadcast_to(value[None], (message.shape[0],) + value.shape)


def keep_kernel(weight, out):
    out[...] = weight[...]


def spread_kernel(near, spread):
    used = spread.shape[2]
    for i in range(spread.shape[0]):
        at = i % 2 * used
        spread[i] = near[:, at : at + used]


def order_kernel(sizes, mine, other, out, arrived):
    x_size, rows, _ = mine.shape
    for ref, c in ((mine, lax.axis_index("c")), (other, 1 - lax.axis_index("c"))):
        for k in range(x_size):
            x = lax.rem(lax.axis_index("x") + k, x_size)
            at = pl.multiple_of((x * 2 + c) * rows, rows)
            arrived[pl.ds(at, rows), :] = ref[k]
    by_arrival = arrival(sizes, arrived.shape[0])
    out[...] = jnp.dot(by_arrival, arrived[...], preferred_element_type=F32).astype(BF16)


def project_kernel(weight, *refs):
    mine, other, qkv_out = refs[:3], refs[3:6], refs[6]
    depth, used = weight.shape
    p, c = lax.axis_index("p"), lax.axis_index("c")
    heads = used // (HD + HALF)
    wide = heads * HD

    for blocks, at_c in ((mine, c), (other, 1 - c)):
        for side, pair in enumerate(blocks):
            columns = used if side == 0 else wide
            to = 0 if side == 0 else HALF + side * HD
            result = jnp.dot(
                pair[...].reshape(2 * BLK, depth), weight[:, :columns], preferred_element_type=F32
            )
            flipped = result.astype(BF16).T
            for j in range(2):
                at_p = p if j == 0 else 1 - p
                lanes = pl.ds(pl.multiple_of((at_c * 2 + at_p) * BLK, BLK), BLK)
                part = flipped[:, j * BLK : (j + 1) * BLK]
                for head in range(heads):
                    qkv_out[head, to : to + HD, lanes] = part[head * HD : (head + 1) * HD]
                    if side == 0:
                        at = wide + (head % 2 * 2 + head // 2) * HALF
                        qkv_out[head, HD : HD + HALF, lanes] = part[at : at + HALF]


def attend_kernel(scale, units, lanes, counts, mine, other, out, scores):
    q_blocks = out.shape[0]
    slots = scores.shape[1]
    core = lax.axis_index("c")

    def attend(keys, values, low, high):
        def one_block(block, room):
            yh, p = block // 2, block % 2
            q_unit = yh * UNITS + 2
            q_lanes = pl.ds(pl.multiple_of((core * 2 + p) * BLK, BLK), BLK)
            query = jnp.concatenate([low[q_unit, :, q_lanes], high[q_unit, :, q_lanes]], axis=0).T
            count = counts[block]

            def tiles(ref, first):
                found = []
                for slot in range(first, first + UNROLL):
                    at = pl.ds(pl.multiple_of(lanes[block, slot], BLK), BLK)
                    found.append(ref[pl.ds(units[block, slot], 2), :, at].reshape(HD, BLK))
                return jnp.concatenate(found, axis=1)

            top = jnp.full((BLK, BLK), -1e30, F32)
            for first in range(0, slots, UNROLL):
                got = jnp.dot(query, tiles(keys, first), preferred_element_type=F32)
                got = got * (scale * LOG2_E)
                for i in range(UNROLL):
                    part = jnp.where(first + i < count, got[:, i * BLK : (i + 1) * BLK], -1e30)
                    scores[room, first + i] = part
                    top = jnp.maximum(top, part)
            top = jnp.max(top, axis=1, keepdims=True)

            total = jnp.zeros((BLK, BLK), F32)
            summed = jnp.zeros((BLK, HD), F32)
            for first in range(0, slots, UNROLL):
                soft = []
                for i in range(UNROLL):
                    part = jnp.exp2(scores[room, first + i] - top)
                    total = total + part
                    soft.append(part.astype(BF16))
                summed = summed + lax.dot_general(
                    jnp.concatenate(soft, axis=1), tiles(values, first), (((1,), (1,)), ((), ())),
                    preferred_element_type=F32,
                )
            total = jnp.sum(total, axis=1, keepdims=True)
            out[block] = (summed / total).T.astype(BF16)

        def several(step, carry):
            for room in range(TOGETHER):
                one_block(step * TOGETHER + room, room)
            return carry

        lax.fori_loop(0, q_blocks // TOGETHER, several, 0)

    @pl.when(core == 0)
    def _():
        attend(mine, other, mine, other)

    @pl.when(core == 1)
    def _():
        attend(other, mine, other, mine)


def mix_kernel(attended, weight, mixed):
    count = attended.shape[0] // 2
    heads = [attended[yh * 2 + p] for p in range(2) for yh in range(count)]
    mixed[...] = lax.dot_general(
        jnp.concatenate(heads, axis=0).T, weight[...], (((1,), (1,)), ((), ())),
        preferred_element_type=F32,
    ).astype(BF16)


def block_lists(neighbours, counts, c, slab, slabs, yh_size):
    ka_size = yh_size * 4
    listed = neighbours.reshape(yh_size * 2, 2, -1)
    listed = lax.dynamic_index_in_dim(listed, c, axis=1, keepdims=False)
    used = lax.dynamic_index_in_dim(counts.reshape(yh_size * 2, 2), c, axis=1, keepdims=False)
    side = (listed // ka_size - slab + 1 + slabs) % slabs
    along = listed % ka_size
    offset = jnp.where(side == 1, 0, jnp.where(side == 0, 3, 5))
    unit = along // 4 * UNITS + offset
    lane = (along % 2 * 2 + along // 2 % 2) * BLK
    is_used = jnp.arange(listed.shape[1])[None, :] < used[:, None]
    return (
        jnp.where(is_used, unit, 0).astype(jnp.int32),
        jnp.where(is_used, lane, 0).astype(jnp.int32),
        used,
    )


def body(features, order, neighbours, counts, qkv_weight, out_weight):
    dev_rows, depth = features.shape
    rows, width = qkv_weight.shape[0], qkv_weight.shape[1] // 3
    z_size, x_size, yh_size = (lax.axis_size(name) for name in ("z", "x", "yh"))
    slabs = z_size * x_size
    c = lax.axis_index("c")
    slab = lax.axis_index("z") * x_size + lax.axis_index("x")
    used_width = width * 3 // 4

    sizes = (z_size, x_size, yh_size)
    near_width = 2 * used_width + width

    with jax.named_scope("weights_near"):
        message, own = pl.pallas_call(
            functools.partial(message_kernel, sizes),
            out_shape=(
                jax.ShapeDtypeStruct((z_size * yh_size, 2, rows, near_width), BF16),
                jax.ShapeDtypeStruct(features.shape, BF16),
            ),
            in_specs=[vmem()] * 4,
            out_specs=(vmem(), vmem()),
            name="message",
        )(order.reshape(1, -1), features, qkv_weight, out_weight.T)

    with jax.named_scope("rows"):
        pair = jnp.stack([own, lax.ppermute(own, "p", ring(2, 1))])
        before = lax.ppermute(pair, ("z", "x"), ring(slabs, 1))
        after = lax.ppermute(pair, ("z", "x"), ring(slabs, -1))

    with jax.named_scope("weights_near"):
        message = message.reshape(-1, rows, near_width)
        near = lax.all_to_all(message, ("z", "yh", "p"), 0, 0, tiled=True)
        near = near.reshape(-1, near_width)

    with jax.named_scope("lists"):
        lists = block_lists(neighbours, counts, c, slab, slabs, yh_size)
        near, lists, _ = lax.optimization_barrier((near, lists, pair))
        unit, lane, used = lists

    with jax.named_scope("weights_far"):
        spread = pl.pallas_call(
            spread_kernel,
            out_shape=jax.ShapeDtypeStruct((x_size * 2, near.shape[0], used_width), BF16),
            in_specs=[vmem()],
            out_specs=vmem(),
            compiler_params=limit(16),
            name="spread",
        )(near)
        weight = lax.all_to_all(spread, ("x", "c"), 0, 0, tiled=True).reshape(depth, -1)
        _, mine = lax.optimization_barrier((spread, (pair, before, after)))
        other = [lax.ppermute(piece, "c", ring(2, 1)) for piece in mine]
        weight = pl.pallas_call(
            keep_kernel,
            out_shape=jax.ShapeDtypeStruct(weight.shape, BF16),
            in_specs=[vmem()],
            out_specs=vmem(),
            compiler_params=limit(16),
            name="keep",
        )(weight)

    with jax.named_scope("project"):
        qkv = pl.pallas_call(
            project_kernel,
            out_shape=jax.ShapeDtypeStruct((yh_size, UNITS * HALF, 4 * dev_rows), BF16),
            in_specs=[vmem()] * 7,
            out_specs=vmem(),
            compiler_params=limit(24),
            name="project",
        )(weight, *mine, *other)
        qkv, near = lax.optimization_barrier((qkv, near))

    with jax.named_scope("heads"):
        mine = lax.all_to_all(qkv, "yh", 0, 0, tiled=True)

    with jax.named_scope("out_weight"):
        near_out = near[:, 2 * used_width :]
        ringed = [near_out] + [
            lax.ppermute(near_out, "x", ring(x_size, -k)) for k in range(1, x_size)
        ]
        ringed = jnp.stack(ringed)
        mine, _ = lax.optimization_barrier((mine, ringed))
        mine = mine.reshape(-1, HALF, 4 * dev_rows)
        ringed_other = lax.ppermute(ringed, "c", ring(2, 1))

    with jax.named_scope("attend"):
        other = lax.ppermute(mine, "c", ring(2, 1))
        slots = -(-neighbours.shape[1] // UNROLL) * UNROLL
        attended = pl.pallas_call(
            functools.partial(attend_kernel, HD ** -0.5),
            out_shape=jax.ShapeDtypeStruct((yh_size * 2, HD, dev_rows), BF16),
            in_specs=[smem()] * 3 + [vmem()] * 2,
            out_specs=vmem(),
            scratch_shapes=[pltpu.VMEM((TOGETHER, slots, BLK, BLK), F32)],
            compiler_params=limit(24),
            name="attend",
        )(unit, lane, used, mine, other)

    with jax.named_scope("return"):
        _, pieces = lax.optimization_barrier((attended, (ringed, ringed_other)))
        attended = lax.all_to_all(attended, ("yh", "p"), 0, 0, tiled=True)

        mix_weight = pl.pallas_call(
            functools.partial(order_kernel, sizes),
            out_shape=jax.ShapeDtypeStruct((depth, width), BF16),
            in_specs=[vmem()] * 2,
            out_specs=vmem(),
            scratch_shapes=[pltpu.VMEM((depth, width), BF16)],
            compiler_params=limit(24),
            name="order",
        )(*pieces)

    with jax.named_scope("mix"):
        return pl.pallas_call(
            mix_kernel,
            out_shape=jax.ShapeDtypeStruct((dev_rows, depth), BF16),
            in_specs=[vmem()] * 2,
            out_specs=vmem(),
            compiler_params=limit(16),
            name="mix",
        )(attended, mix_weight)


def solution(mesh):
    pb_size, ka_size = mesh.shape["pb"], mesh.shape["ka"]
    shape = (pb_size // CHIPS_X, CHIPS_X, ka_size // CORES // 2, 2, CORES)
    fine = Mesh(mesh.devices.reshape(shape), ALL)
    return jax.shard_map(
        body,
        mesh=fine,
        in_specs=(
            P(ALL, None),
            P(ALL),
            P(("z", "x"), None),
            P(("z", "x")),
            P(ALL, None),
            P(None, ALL),
        ),
        out_specs=P(ALL, None),
        check_vma=False,
    )
```

```python
import functools

import jax
import jax.numpy as jnp
from jax import lax
from jax.experimental import pallas as pl
from jax.experimental.pallas import tpu as pltpu
from jax.sharding import Mesh, PartitionSpec as P

HD = 64
HALF = HD // 2
BLK = 128
UNROLL = 4
TOGETHER = 8
CHIPS_X = 4
CORES = 2
LOG2_E = 1.4426950408889634
ALL = ("z", "x", "yh", "p", "c")
BF16 = jnp.bfloat16
F32 = jnp.float32

UNITS = 7


def vmem():
    return pl.BlockSpec(memory_space=pltpu.VMEM)


def smem():
    return pl.BlockSpec(memory_space=pltpu.SMEM)


def limit(mib):
    return pltpu.CompilerParams(vmem_limit_bytes=mib << 20)


def ring(size, step):
    return [(i, (i + step) % size) for i in range(size)]


def arrival(sizes, depth):
    z_size, x_size, yh_size = sizes
    rows = depth // (z_size * x_size * yh_size * 4)
    at = lax.broadcasted_iota(jnp.int32, (1, depth), 1)
    row, at = at % rows, at // rows
    p, at = at % 2, at // 2
    yh, at = at % yh_size, at // yh_size
    z, at = at % z_size, at // z_size
    c, x = at % 2, at // 2
    natural = (((z * x_size + x) * yh_size + yh) * 4 + p * 2 + c) * rows + row
    index = lax.broadcasted_iota(jnp.int32, (depth, depth), 0)
    return jnp.where(index == natural, 1.0, 0.0).astype(BF16)


def message_kernel(sizes, order, features, qkv, out_t, message, own):
    position = lax.broadcasted_iota(jnp.int32, (order.shape[1],) * 2, 0)
    picks = jnp.where(position == order[...], 1.0, 0.0).T.astype(BF16)
    found = jnp.dot(picks, features[...], preferred_element_type=F32).astype(BF16)
    by_arrival = arrival(sizes, features.shape[1])
    own[...] = jnp.dot(found, by_arrival, preferred_element_type=F32).astype(BF16)
    rows, width = qkv.shape[0], qkv.shape[1] // 3
    lane = lax.broadcasted_iota(jnp.int32, (rows, BLK), 1)
    first = lane // HALF % 2 == 0
    for p in range(2):
        parts = []
        at = p * width // 2
        left = qkv[:, at : at + BLK].astype(F32)
        right = qkv[:, at + BLK : at + 2 * BLK].astype(F32)
        for c in range(2):
            if c == 0:
                query = jnp.where(first, left, pltpu.roll(right, HALF, 1))
            else:
                query = jnp.where(first, pltpu.roll(left, BLK - HALF, 1), right)
            from_kv = (1 + c) * width + p * width // 2
            parts += [qkv[:, from_kv : from_kv + width // 2], query.astype(BF16)]
        value = jnp.concatenate(parts + [out_t[...]], axis=-1)
        message[:, p] = jnp.broadcast_to(value[None], (message.shape[0],) + value.shape)


def keep_kernel(weight, out):
    out[...] = weight[...]


def spread_kernel(near, spread):
    used = spread.shape[2]
    for i in range(spread.shape[0]):
        at = i % 2 * used
        spread[i] = near[:, at : at + used]


def order_kernel(sizes, mine, other, out, arrived):
    x_size, rows, _ = mine.shape
    for ref, c in ((mine, lax.axis_index("c")), (other, 1 - lax.axis_index("c"))):
        for k in range(x_size):
            x = lax.rem(lax.axis_index("x") + k, x_size)
            at = pl.multiple_of((x * 2 + c) * rows, rows)
            arrived[pl.ds(at, rows), :] = ref[k]
    by_arrival = arrival(sizes, arrived.shape[0])
    out[...] = jnp.dot(by_arrival, arrived[...], preferred_element_type=F32).astype(BF16)


def project_kernel(weight, *refs):
    mine, other, qkv_out = refs[:3], refs[3:6], refs[6]
    depth, used = weight.shape
    p, c = lax.axis_index("p"), lax.axis_index("c")
    heads = used // (HD + HALF)
    wide = heads * HD

    for blocks, at_c in ((mine, c), (other, 1 - c)):
        for side, pair in enumerate(blocks):
            columns = used if side == 0 else wide
            to = 0 if side == 0 else HALF + side * HD
            result = jnp.dot(
                pair[...].reshape(2 * BLK, depth), weight[:, :columns], preferred_element_type=F32
            )
            flipped = result.astype(BF16).T
            for j in range(2):
                at_p = p if j == 0 else 1 - p
                lanes = pl.ds(pl.multiple_of((at_c * 2 + at_p) * BLK, BLK), BLK)
                part = flipped[:, j * BLK : (j + 1) * BLK]
                for head in range(heads):
                    qkv_out[head, to : to + HD, lanes] = part[head * HD : (head + 1) * HD]
                    if side == 0:
                        at = wide + (head % 2 * 2 + head // 2) * HALF
                        qkv_out[head, HD : HD + HALF, lanes] = part[at : at + HALF]


def attend_kernel(scale, units, lanes, counts, mine, other, out, scores):
    q_blocks = out.shape[0]
    slots = scores.shape[1]
    core = lax.axis_index("c")

    def attend(keys, values, low, high):
        def one_block(block, room):
            yh, p = block // 2, block % 2
            q_unit = yh * UNITS + 2
            q_lanes = pl.ds(pl.multiple_of((core * 2 + p) * BLK, BLK), BLK)
            query = jnp.concatenate([low[q_unit, :, q_lanes], high[q_unit, :, q_lanes]], axis=0).T
            count = counts[block]

            def tiles(ref, first):
                found = []
                for slot in range(first, first + UNROLL):
                    at = pl.ds(pl.multiple_of(lanes[block, slot], BLK), BLK)
                    found.append(ref[pl.ds(units[block, slot], 2), :, at].reshape(HD, BLK))
                return jnp.concatenate(found, axis=1)

            top = jnp.full((BLK, BLK), -1e30, F32)
            for first in range(0, slots, UNROLL):
                got = jnp.dot(query, tiles(keys, first), preferred_element_type=F32)
                got = got * (scale * LOG2_E)
                for i in range(UNROLL):
                    part = jnp.where(first + i < count, got[:, i * BLK : (i + 1) * BLK], -1e30)
                    scores[room, first + i] = part
                    top = jnp.maximum(top, part)
            top = jnp.max(top, axis=1, keepdims=True)

            total = jnp.zeros((BLK, BLK), F32)
            summed = jnp.zeros((BLK, HD), F32)
            for first in range(0, slots, UNROLL):
                soft = []
                for i in range(UNROLL):
                    part = jnp.exp2(scores[room, first + i] - top)
                    total = total + part
                    soft.append(part.astype(BF16))
                summed = summed + lax.dot_general(
                    jnp.concatenate(soft, axis=1), tiles(values, first), (((1,), (1,)), ((), ())),
                    preferred_element_type=F32,
                )
            total = jnp.sum(total, axis=1, keepdims=True)
            out[block] = (summed / total).T.astype(BF16)

        def several(step, carry):
            for room in range(TOGETHER):
                one_block(step * TOGETHER + room, room)
            return carry

        lax.fori_loop(0, q_blocks // TOGETHER, several, 0)

    @pl.when(core == 0)
    def _():
        attend(mine, other, mine, other)

    @pl.when(core == 1)
    def _():
        attend(other, mine, other, mine)


def mix_kernel(attended, weight, mixed):
    count = attended.shape[0] // 2
    heads = [attended[yh * 2 + p] for p in range(2) for yh in range(count)]
    mixed[...] = lax.dot_general(
        jnp.concatenate(heads, axis=0).T, weight[...], (((1,), (1,)), ((), ())),
        preferred_element_type=F32,
    ).astype(BF16)


def block_lists(neighbours, counts, c, slab, slabs, yh_size):
    ka_size = yh_size * 4
    listed = neighbours.reshape(yh_size * 2, 2, -1)
    listed = lax.dynamic_index_in_dim(listed, c, axis=1, keepdims=False)
    used = lax.dynamic_index_in_dim(counts.reshape(yh_size * 2, 2), c, axis=1, keepdims=False)
    side = (listed // ka_size - slab + 1 + slabs) % slabs
    along = listed % ka_size
    offset = jnp.where(side == 1, 0, jnp.where(side == 0, 3, 5))
    unit = along // 4 * UNITS + offset
    lane = (along % 2 * 2 + along // 2 % 2) * BLK
    is_used = jnp.arange(listed.shape[1])[None, :] < used[:, None]
    return (
        jnp.where(is_used, unit, 0).astype(jnp.int32),
        jnp.where(is_used, lane, 0).astype(jnp.int32),
        used,
    )


def body(features, order, neighbours, counts, qkv_weight, out_weight):
    dev_rows, depth = features.shape
    rows, width = qkv_weight.shape[0], qkv_weight.shape[1] // 3
    z_size, x_size, yh_size = (lax.axis_size(name) for name in ("z", "x", "yh"))
    slabs = z_size * x_size
    c = lax.axis_index("c")
    slab = lax.axis_index("z") * x_size + lax.axis_index("x")
    used_width = width * 3 // 4

    sizes = (z_size, x_size, yh_size)
    near_width = 2 * used_width + width

    with jax.named_scope("weights_near"):
        message, own = pl.pallas_call(
            functools.partial(message_kernel, sizes),
            out_shape=(
                jax.ShapeDtypeStruct((z_size * yh_size, 2, rows, near_width), BF16),
                jax.ShapeDtypeStruct(features.shape, BF16),
            ),
            in_specs=[vmem()] * 4,
            out_specs=(vmem(), vmem()),
            name="message",
        )(order.reshape(1, -1), features, qkv_weight, out_weight.T)

    with jax.named_scope("rows"):
        pair = jnp.stack([own, lax.ppermute(own, "p", ring(2, 1))])
        before = lax.ppermute(pair, ("z", "x"), ring(slabs, 1))
        after = lax.ppermute(pair, ("z", "x"), ring(slabs, -1))

    with jax.named_scope("weights_near"):
        message = message.reshape(-1, rows, near_width)
        near = lax.all_to_all(message, ("z", "yh", "p"), 0, 0, tiled=True)
        near = near.reshape(-1, near_width)

    with jax.named_scope("lists"):
        lists = block_lists(neighbours, counts, c, slab, slabs, yh_size)
        near, lists, _ = lax.optimization_barrier((near, lists, pair))
        unit, lane, used = lists

    with jax.named_scope("weights_far"):
        spread = pl.pallas_call(
            spread_kernel,
            out_shape=jax.ShapeDtypeStruct((x_size * 2, near.shape[0], used_width), BF16),
            in_specs=[vmem()],
            out_specs=vmem(),
            compiler_params=limit(16),
            name="spread",
        )(near)
        weight = lax.all_to_all(spread, ("x", "c"), 0, 0, tiled=True).reshape(depth, -1)
        _, mine = lax.optimization_barrier((spread, (pair, before, after)))
        other = [lax.ppermute(piece, "c", ring(2, 1)) for piece in mine]
        weight = pl.pallas_call(
            keep_kernel,
            out_shape=jax.ShapeDtypeStruct(weight.shape, BF16),
            in_specs=[vmem()],
            out_specs=vmem(),
            compiler_params=limit(16),
            name="keep",
        )(weight)

    with jax.named_scope("project"):
        qkv = pl.pallas_call(
            project_kernel,
            out_shape=jax.ShapeDtypeStruct((yh_size, UNITS * HALF, 4 * dev_rows), BF16),
            in_specs=[vmem()] * 7,
            out_specs=vmem(),
            compiler_params=limit(24),
            name="project",
        )(weight, *mine, *other)
        qkv, near = lax.optimization_barrier((qkv, near))

    with jax.named_scope("heads"):
        mine = lax.all_to_all(qkv, "yh", 0, 0, tiled=True)

    with jax.named_scope("out_weight"):
        near_out = near[:, 2 * used_width :]
        ringed = [near_out] + [
            lax.ppermute(near_out, "x", ring(x_size, -k)) for k in range(1, x_size)
        ]
        ringed = jnp.stack(ringed)
        ringed_other = lax.ppermute(ringed, "c", ring(2, 1))
        mine, _ = lax.optimization_barrier((mine, ringed_other))
        mine = mine.reshape(-1, HALF, 4 * dev_rows)

    with jax.named_scope("attend"):
        other = lax.ppermute(mine, "c", ring(2, 1))
        slots = -(-neighbours.shape[1] // UNROLL) * UNROLL
        attended = pl.pallas_call(
            functools.partial(attend_kernel, HD ** -0.5),
            out_shape=jax.ShapeDtypeStruct((yh_size * 2, HD, dev_rows), BF16),
            in_specs=[smem()] * 3 + [vmem()] * 2,
            out_specs=vmem(),
            scratch_shapes=[pltpu.VMEM((TOGETHER, slots, BLK, BLK), F32)],
            compiler_params=limit(24),
            name="attend",
        )(unit, lane, used, mine, other)

    with jax.named_scope("return"):
        _, pieces = lax.optimization_barrier((attended, (ringed, ringed_other)))
        attended = lax.all_to_all(attended, ("yh", "p"), 0, 0, tiled=True)

        mix_weight = pl.pallas_call(
            functools.partial(order_kernel, sizes),
            out_shape=jax.ShapeDtypeStruct((depth, width), BF16),
            in_specs=[vmem()] * 2,
            out_specs=vmem(),
            scratch_shapes=[pltpu.VMEM((depth, width), BF16)],
            compiler_params=limit(24),
            name="order",
        )(*pieces)

    with jax.named_scope("mix"):
        return pl.pallas_call(
            mix_kernel,
            out_shape=jax.ShapeDtypeStruct((dev_rows, depth), BF16),
            in_specs=[vmem()] * 2,
            out_specs=vmem(),
            compiler_params=limit(16),
            name="mix",
        )(attended, mix_weight)


def solution(mesh):
    pb_size, ka_size = mesh.shape["pb"], mesh.shape["ka"]
    shape = (pb_size // CHIPS_X, CHIPS_X, ka_size // CORES // 2, 2, CORES)
    fine = Mesh(mesh.devices.reshape(shape), ALL)
    return jax.shard_map(
        body,
        mesh=fine,
        in_specs=(
            P(ALL, None),
            P(ALL),
            P(("z", "x"), None),
            P(("z", "x")),
            P(ALL, None),
            P(None, ALL),
        ),
        out_specs=P(ALL, None),
        check_vma=False,
    )
```
